256 devices in a mesh: ctx: 64 (over x, z, y_hi), tp: 4 (over y_lo, core).
Axes of the slice: x: 4, y: 4 (y_hi: 2, y_lo: 2; y = y_hi * 2 + y_lo), z: 8, core: 2. Of those that a mesh axis runs over, the one named last changes fastest.
Arguments:
- tokens: bfloat16 [16384, 8192], P('ctx'), may hold values from -6 to 6
- select_index: int32 [2048], P('ctx'), may hold values from 0 to 255, as said below
- valid_count: int32 [64], replicated, may hold values from 4 to 32, as said below
- queries: bfloat16 [2048, 4096], P('ctx', 'tp'), may hold values from -160 to 160
- key_matrix: bfloat16 [8192, 512], P('ctx', 'tp'), may hold values from -0.0625 to 0.0625
- value_matrix: bfloat16 [8192, 512], P('ctx', 'tp'), may hold values from -0.0625 to 0.0625
- out_grad: bfloat16 [2048, 4096], P('ctx', 'tp'), may hold values from -6 to 6
Outputs:
- attended: bfloat16 [2048, 4096], P('ctx', 'tp')
- query_gradient: bfloat16 [2048, 4096], P('ctx', 'tp')
- token_grad: bfloat16 [16384, 8192], P('ctx', 'tp')
- key_weight_grad: bfloat16 [8192, 512], P('ctx', 'tp')
- value_weight_grad: bfloat16 [8192, 512], P('ctx', 'tp')
The draws below stay inside these ranges and needn't reach their ends.
Inputs may be any that keep to these rules, and one draw needn't show every extreme that they name: `select_index`: within one shard the offsets of all 32 slots are distinct, and those of the first valid_count slots rise. `valid_count`: some shard holds exactly 32 live slots.
All inputs are finite; a program needn't handle non-finite values.
Results may differ from the reference program's by a relative error of at most 0.023.
The reference program's roundings to bfloat16 on the way count: a program that leaves them out, or rounds other values in their place, can miss the bound.
Values may be sent and summed in bfloat16 or wider, within the bound.
A program may use at most 64 MiB of HBM per device.

```python
import math
import jax
import jax.numpy as jnp
from jax import lax

MODEL_WIDTH = 8192
HEAD_WIDTH = 128
KEY_VALUE_HEADS = 4
HEADS_PER_KEY = 8
SHARD = 256
SLOT_LIMIT = 32
HQ = 32
SEQ = 16384
ROUTED_KEYS = 2048


def draw_order(subkey):
    return jax.random.permutation(subkey, SHARD)


def selection(key):
    shards = ROUTED_KEYS // SLOT_LIMIT
    counts = jax.random.randint(jax.random.fold_in(key, 11), (shards,), SLOT_LIMIT // 8, 3 * SLOT_LIMIT // 4 + 1)
    busiest = jax.random.randint(jax.random.fold_in(key, 12), (), 0, shards)
    counts = jnp.where(jnp.arange(shards) == busiest, SLOT_LIMIT, counts).astype(jnp.int32)
    subkeys = jax.random.split(jax.random.fold_in(key, 13), shards)
    orders = jax.vmap(draw_order)(subkeys)[:, :SLOT_LIMIT].astype(jnp.int32)
    is_live = jnp.arange(SLOT_LIMIT)[None, :] < counts[:, None]
    ranked = jnp.sort(jnp.where(is_live, orders, orders + SHARD), axis=1)
    offsets = jnp.where(ranked >= SHARD, ranked - SHARD, ranked)
    return (counts, offsets.reshape(ROUTED_KEYS).astype(jnp.int32))


def draw_valid_count(key, part):
    return selection(key)[0]


def draw_select_index(key, part):
    return selection(key)[1]


def draw_queries(key, part):
    random_perturb = jax.random.normal(jax.random.fold_in(key, 21), (ROUTED_KEYS, KEY_VALUE_HEADS * HEADS_PER_KEY * HEAD_WIDTH), jnp.float32)
    random_perturb = jnp.clip(random_perturb, -6.0, 6.0)
    return random_perturb.astype(jnp.bfloat16)


def levels(own_key, extent, cuts, least, top_value):
    def one(dim, blocks):
        draws = jax.random.uniform(jax.random.fold_in(jax.random.fold_in(own_key, 6), dim), (blocks,), jnp.float32, least / len(cuts), top_value / len(cuts))
        return jnp.repeat(jnp.exp(draws), extent[dim] // blocks).reshape((-1,) + (1,) * (len(extent) - dim - 1))

    loudness = one(*cuts[0])
    for cut in cuts[1:]:
        loudness = loudness * one(*cut)
    return loudness


def centred(own_key, dims, scale, limit, cuts=(), kind=jnp.bfloat16):
    values = jax.random.normal(own_key, dims, jnp.float32) * scale
    if len(cuts) > 0:
        values = levels(own_key, dims, cuts, -0.22, 0.18) * values
    return jnp.clip(values, min=-limit, max=limit).astype(kind)


def setup_inputs(seed: int = 0) -> dict:
    key_of = jax.random.split(jax.random.key(seed), 8)
    tokens = centred(key_of[0], (SEQ, MODEL_WIDTH), 1.0, 6.0, ((0, 64),))
    select_index = draw_select_index(jax.random.fold_in(key_of[7], 71), 0)
    valid_count = draw_valid_count(jax.random.fold_in(key_of[7], 71), 0)
    queries = draw_queries(jax.random.fold_in(key_of[7], 71), 0)
    key_matrix = centred(key_of[4], (MODEL_WIDTH, KEY_VALUE_HEADS * HEAD_WIDTH), MODEL_WIDTH ** -0.5, 0.0625, ((0, 64), (1, 4)))
    value_matrix = centred(key_of[5], (MODEL_WIDTH, KEY_VALUE_HEADS * HEAD_WIDTH), MODEL_WIDTH ** -0.5, 0.0625, ((0, 64), (1, 4)))
    out_grad = centred(key_of[6], (ROUTED_KEYS, HQ * HEAD_WIDTH), 1.0, 6.0, ((0, 64), (1, 4)))
    return {"tokens": tokens, "select_index": select_index, "valid_count": valid_count, "queries": queries, "key_matrix": key_matrix, "value_matrix": value_matrix, "out_grad": out_grad}


def reference(tokens, select_index, valid_count, queries, key_matrix, value_matrix, out_grad):
    score_scale = 1.0 / math.sqrt(HEAD_WIDTH)
    key_value_width = KEY_VALUE_HEADS * HEAD_WIDTH
    key_ids = jnp.arange(ROUTED_KEYS, dtype=jnp.int32)
    key_shard = key_ids // SLOT_LIMIT
    slot_in = key_ids % SLOT_LIMIT
    key_live = slot_in < jnp.take(valid_count, key_shard)
    row_ids = (key_shard * SHARD + select_index).astype(jnp.int32)
    query_pos = jnp.where(key_live, row_ids, key_shard * SHARD + SHARD)
    picked = jnp.take(tokens, row_ids, axis=0)
    key_vectors = jnp.dot(picked, key_matrix, preferred_element_type=jnp.float32).astype(jnp.bfloat16)
    value_vectors = jnp.dot(picked, value_matrix, preferred_element_type=jnp.float32).astype(jnp.bfloat16)
    heads_of_key = key_vectors.astype(jnp.float32).reshape(ROUTED_KEYS, KEY_VALUE_HEADS, HEAD_WIDTH)
    heads_of_value = value_vectors.astype(jnp.float32).reshape(ROUTED_KEYS, KEY_VALUE_HEADS, HEAD_WIDTH)
    gradient_rows = jnp.where(key_live[:, None], out_grad, jnp.zeros_like(out_grad))

    def per_shard(carried, shard):
        key_accumulator, value_accumulator = carried
        leading_item = (shard * SLOT_LIMIT).astype(jnp.int32)
        query_block = lax.dynamic_slice_in_dim(queries, leading_item, SLOT_LIMIT, 0).astype(jnp.float32).reshape(SLOT_LIMIT, KEY_VALUE_HEADS, HEADS_PER_KEY, HEAD_WIDTH)
        gradient_block = lax.dynamic_slice_in_dim(gradient_rows, leading_item, SLOT_LIMIT, 0).astype(jnp.float32).reshape(SLOT_LIMIT, KEY_VALUE_HEADS, HEADS_PER_KEY, HEAD_WIDTH)
        live_blk = lax.dynamic_slice_in_dim(key_live, leading_item, SLOT_LIMIT, 0)
        pos_blk = lax.dynamic_slice_in_dim(query_pos, leading_item, SLOT_LIMIT, 0)
        visible = key_live[None, :] & (row_ids[None, :] <= pos_blk[:, None])
        scores = jnp.einsum('qkgd,nkd->kgqn', query_block, heads_of_key) * score_scale
        scores = jnp.where(visible[None, None], scores, -jnp.inf)
        log_total = jax.nn.logsumexp(scores, axis=-1)
        probs = jnp.exp(scores - log_total[..., None])
        weight_matrices = lax.optimization_barrier(probs.astype(jnp.bfloat16)).astype(jnp.float32)
        output_single = jnp.einsum('kgqn,nkd->qkgd', weight_matrices, heads_of_value)
        output_single = jnp.where(live_blk[:, None, None, None], output_single, 0.0).astype(jnp.bfloat16)
        out_dot = jnp.transpose(lax.optimization_barrier(jnp.sum(gradient_block * output_single.astype(jnp.float32), axis=-1)), (1, 2, 0))
        grad_probs = jnp.einsum('qkgd,nkd->kgqn', gradient_block, heads_of_value)
        score_gradient = probs * (grad_probs - out_dot[..., None]) * score_scale
        score_gradient = lax.optimization_barrier(score_gradient.astype(jnp.bfloat16)).astype(jnp.float32)
        query_gradient = jnp.einsum('kgqn,nkd->qkgd', score_gradient, heads_of_key).astype(jnp.bfloat16)
        key_accumulator = key_accumulator + jnp.einsum('kgqn,qkgd->nkd', score_gradient, query_block)
        value_accumulator = value_accumulator + jnp.einsum('kgqn,qkgd->nkd', weight_matrices, gradient_block)
        return ((key_accumulator, value_accumulator), (output_single.reshape(SLOT_LIMIT, KEY_VALUE_HEADS * HEADS_PER_KEY * HEAD_WIDTH), query_gradient.reshape(SLOT_LIMIT, KEY_VALUE_HEADS * HEADS_PER_KEY * HEAD_WIDTH)))
    empty_accumulator = jnp.zeros((ROUTED_KEYS, KEY_VALUE_HEADS, HEAD_WIDTH), jnp.float32)
    (key_accumulator, value_accumulator), (output_rows, query_gradient_rows) = lax.scan(per_shard, (empty_accumulator, empty_accumulator), jnp.arange(ROUTED_KEYS // SLOT_LIMIT, dtype=jnp.int32))
    attended = output_rows.reshape(ROUTED_KEYS, KEY_VALUE_HEADS * HEADS_PER_KEY * HEAD_WIDTH)
    query_gradient = query_gradient_rows.reshape(ROUTED_KEYS, KEY_VALUE_HEADS * HEADS_PER_KEY * HEAD_WIDTH)
    key_grads = key_accumulator.reshape(ROUTED_KEYS, key_value_width).astype(jnp.bfloat16)
    value_grads = value_accumulator.reshape(ROUTED_KEYS, key_value_width).astype(jnp.bfloat16)
    key_weight_grad = jnp.dot(picked.T, key_grads, preferred_element_type=jnp.float32).astype(jnp.bfloat16)
    value_weight_grad = jnp.dot(picked.T, value_grads, preferred_element_type=jnp.float32).astype(jnp.bfloat16)
    row_grad = jnp.dot(key_grads, key_matrix.T, preferred_element_type=jnp.float32) + jnp.dot(value_grads, value_matrix.T, preferred_element_type=jnp.float32)
    row_grad = jnp.where(key_live[:, None], row_grad, 0.0)
    token_grad = jnp.zeros(tokens.shape, jnp.float32).at[row_ids].set(row_grad).astype(jnp.bfloat16)
    return (attended, query_gradient, token_grad, key_weight_grad, value_weight_grad)
```

```python
import math

import jax
import jax.numpy as jnp
from jax import lax
from jax.experimental import pallas as pl
from jax.experimental.pallas import tpu as pltpu
from jax.sharding import PartitionSpec as P

NX, NZ, NY = 4, 8, 2
HEAD = 128
SLOTS = 32
KV = 2 * HEAD
HEADS = 8
ROWS = 256
MODEL = 8192
PER_X = NZ * NY
CHUNK = PER_X * SLOTS
QROWS = HEADS * SLOTS
SCALE = 1.0 / math.sqrt(HEAD)
NEG = -1e30
BF = jnp.bfloat16
F32 = jnp.float32
ZORDER = (4, 3, 5, 2, 6, 1, 7)
ARRIVE = (1, 7, 2, 6, 3, 5, 4)


def dot(a, b, ca, cb):
    return lax.dot_general(a, b, (((ca,), (cb,)), ((), ())), preferred_element_type=F32)


def kernel(
    tok_hbm, sel_ref, vc_ref, q_ref, wk_ref, wv_ref, g_ref,
    att_ref, dq_ref, tg_ref, kwg_ref, vwg_ref,
    tok, pz, xz, wg, pf, pr, kv, s_ref, qs, gs, tf, tb, hl, hr, cl, cr, ub, zr, vs, yr, gz,
    wb, wf, whl, whr, wcl, wcr, wyb, wyr, rsb, rsr, rf, ryb, ryr, tz, tr,
    tok_sem, z_send, z_recv, x_send, x_recv, ag_send, ag_recv,
):
    c = lax.axis_index("ctx")
    t = lax.axis_index("tp")
    x = c // PER_X
    z = (c // NY) % NZ
    y = c % NY
    core = t % 2
    ylo = t // 2
    right = (x + 1) % NX
    left = (x + NX - 1) % NX

    def at(xx, zz, yy):
        return {"ctx": (xx * NZ + zz) * NY + yy, "tp": t}

    def zpeer(d):
        return at(x, (z + d) % NZ, y)

    to_right = at(right, z, y)
    to_left = at(left, z, y)
    to_y = at(x, z, 1 - y)
    to_sib = {"ctx": c, "tp": 2 * ylo + 1 - core}
    to_ylo = {"ctx": c, "tp": 2 * (1 - ylo) + core}

    started = []

    def copy(src, dst, ssem, rsem, dev):
        return pltpu.make_async_remote_copy(
            src_ref=src, dst_ref=dst, send_sem=ssem, recv_sem=rsem,
            device_id=dev, device_id_type=pl.DeviceIdType.MESH,
        )

    def send(src, dst, ssem, rsem, dev):
        cp = copy(src, dst, ssem, rsem, dev)
        cp.start()
        started.append(cp)

    def arrived(dst, rsem, dev):
        copy(dst, dst, rsem, rsem, dev).wait_recv()

    half_cols = 2 * NZ * KV
    tok_cp = pltpu.make_async_copy(
        tok_hbm.at[:, pl.ds(pl.multiple_of(core * half_cols, half_cols), half_cols)], tok, tok_sem
    )
    tok_cp.start()

    barrier = pltpu.get_barrier_semaphore()
    partners = [zpeer(d) for d in range(1, NZ)] + [to_right, to_left, to_y, to_sib, to_ylo]
    for dev in partners:
        pl.semaphore_signal(barrier, inc=1, device_id=dev, device_id_type=pl.DeviceIdType.MESH)

    wg[x, y, :, 0:HEAD] = wk_ref[...]
    wg[x, y, :, HEAD:KV] = wv_ref[...]

    sel_row = jnp.broadcast_to(sel_ref[...], (SLOTS, SLOTS))
    i0 = lax.broadcasted_iota(jnp.int32, (SLOTS, SLOTS), 0)
    i1 = lax.broadcasted_iota(jnp.int32, (SLOTS, SLOTS), 1)
    sel_col = jnp.sum(jnp.where(i0 == i1, sel_row, 0), axis=1, keepdims=True)
    hot = jnp.where(
        lax.broadcasted_iota(jnp.int32, (SLOTS, ROWS), 1) == sel_col, 1.0, 0.0
    ).astype(BF)
    vc = vc_ref[...]
    own_count = jnp.sum(
        jnp.where(lax.broadcasted_iota(jnp.int32, vc.shape, 1) == c, vc, 0), axis=1, keepdims=True
    )
    live_col = lax.broadcasted_iota(jnp.int32, (SLOTS, 1), 0) < own_count
    live = jnp.where(live_col, 1.0, 0.0)
    qpos = jnp.where(live_col, sel_col, ROWS).astype(F32)
    qpos_all = jnp.concatenate([qpos] * HEADS, axis=0)
    for h in range(HEADS):
        qs[h * SLOTS:(h + 1) * SLOTS, :] = q_ref[:, h * HEAD:(h + 1) * HEAD]
        gs[h * SLOTS:(h + 1) * SLOTS, :] = (
            g_ref[:, h * HEAD:(h + 1) * HEAD].astype(F32) * live
        ).astype(BF)

    pl.semaphore_wait(barrier, len(partners))

    ws, wr = x_send.at[0], x_recv.at[0]
    send(wg.at[x, y], wg.at[x, y], ws.at[0], wr.at[0], to_y)
    send(wg.at[x, y], wg.at[x, y], ws.at[1], wr.at[1], to_right)
    send(wg.at[x, y], wg.at[x, y], ws.at[2], wr.at[2], to_left)

    tok_cp.wait()
    for zt in range(NZ):
        for k in range(2):
            c0 = k * NZ * KV + zt * KV
            pz[zt, k] = dot(hot, tok[:, c0:c0 + KV], 1, 0).astype(BF)
    for d in ZORDER:
        send(
            pz.at[(z + d) % NZ], xz.at[pl.ds(2 * core, 2), z],
            z_send.at[0, d], z_recv.at[0, d], zpeer(d),
        )
    xz[pl.ds(2 * core, 2), z] = pz[z]
    send(
        pz.at[z], xz.at[pl.ds(2 * core, 2), z], z_send.at[1, 0], z_recv.at[1, 0], to_sib
    )

    arrived(wg.at[x, 1 - y], wr.at[0], to_y)
    send(wg.at[x, 1 - y], wg.at[x, 1 - y], ws.at[3], wr.at[3], to_right)
    send(wg.at[x, 1 - y], wg.at[x, 1 - y], ws.at[4], wr.at[4], to_left)

    for d in ARRIVE:
        zs = (z + NZ - d) % NZ
        mine = xz.at[pl.ds(2 * core, 2), zs]
        arrived(mine, z_recv.at[0, d], zpeer(d))
        send(mine, mine, z_send.at[1, d], z_recv.at[1, d], to_sib)

    arrived(wg.at[left, y], wr.at[1], to_left)
    arrived(wg.at[left, 1 - y], wr.at[3], to_left)
    send(wg.at[left, 0], wg.at[left, 0], ws.at[5], wr.at[5], to_right)
    arrived(wg.at[right, y], wr.at[2], to_right)
    arrived(wg.at[right, 1 - y], wr.at[4], to_right)
    send(wg.at[right, 1], wg.at[right, 1], ws.at[6], wr.at[6], to_left)
    for d in (0,) + ARRIVE:
        zs = (z + NZ - d) % NZ
        arrived(xz.at[pl.ds(2 * (1 - core), 2), zs], z_recv.at[1, d], to_sib)
    far = (x + 2) % NX
    arrived(wg.at[far, 0], wr.at[5], to_left)
    arrived(wg.at[far, 1], wr.at[6], to_right)

    acc = jnp.zeros((NZ * SLOTS, KV), F32)
    for xx in range(NX):
        acc = acc + dot(
            xz[xx].reshape(NZ * SLOTS, KV), wg[xx].reshape(NY * HEAD, KV), 1, 0
        )
    pf[...] = acc.reshape(NZ, SLOTS, KV)
    for d in ZORDER:
        send(pf.at[(z + d) % NZ], pr.at[z], z_send.at[2, d], z_recv.at[2, d], zpeer(d))
    total = pf[z]
    for d in ARRIVE:
        zs = (z + NZ - d) % NZ
        arrived(pr.at[zs], z_recv.at[2, d], zpeer(d))
        total = total + pr[zs]
    kv[c] = total.astype(BF)

    send(kv.at[c], kv.at[c], z_send.at[3, 0], z_recv.at[3, 0], to_y)
    peer_c = (x * NZ + z) * NY + 1 - y
    arrived(kv.at[peer_c], z_recv.at[3, 0], to_y)

    def pair(xx, zz):
        return kv.at[pl.ds((xx * NZ + zz) * NY, NY)]

    def one(xx, zz, yy):
        return kv.at[(xx * NZ + zz) * NY + yy]

    for d in ZORDER:
        send(pair(x, z), pair(x, z), z_send.at[3, d], z_recv.at[3, d], zpeer(d))
    for d in (0,) + ARRIVE:
        zs = (z + NZ - d) % NZ
        if d:
            arrived(pair(x, zs), z_recv.at[3, d], zpeer(d))
        send(pair(x, zs), pair(x, zs), ag_send.at[0, d], ag_recv.at[0, d], to_right)
        send(pair(x, zs), pair(x, zs), ag_send.at[1, d], ag_recv.at[1, d], to_left)
    for d in (0,) + ARRIVE:
        zs = (z + NZ - d) % NZ
        arrived(pair(left, zs), ag_recv.at[0, d], to_left)
        send(one(left, zs, 0), one(left, zs, 0), ag_send.at[2, d], ag_recv.at[2, d], to_right)
        arrived(pair(right, zs), ag_recv.at[1, d], to_right)
        send(one(right, zs, 1), one(right, zs, 1), ag_send.at[3, d], ag_recv.at[3, d], to_left)
    for d in (0,) + ARRIVE:
        zs = (z + NZ - d) % NZ
        arrived(one(far, zs, 0), ag_recv.at[2, d], to_left)
        arrived(one(far, zs, 1), ag_recv.at[3, d], to_right)

    vc8 = jnp.broadcast_to(vc.astype(F32), (8, NX * PER_X)).astype(BF)
    sel8 = jnp.broadcast_to(sel_ref[...].astype(F32), (8, SLOTS)).astype(BF)
    jslot = lax.broadcasted_iota(jnp.int32, (SLOTS, CHUNK), 1) % SLOTS
    spread = jnp.where(jslot == lax.broadcasted_iota(jnp.int32, (SLOTS, CHUNK), 0), 1.0, 0.0)
    sel_keys = dot(sel8, spread.astype(BF), 1, 0)[0:1]
    queries = qs[...]
    grads = gs[...]

    def chunk_of(r):
        return (x + r) % NX

    def keys_of(r):
        return kv[pl.ds(chunk_of(r) * PER_X, PER_X), :, 0:HEAD].reshape(CHUNK, HEAD)

    def values_of(r):
        return kv[pl.ds(chunk_of(r) * PER_X, PER_X), :, HEAD:KV].reshape(CHUNK, HEAD)

    top = jnp.full((QROWS, 1), NEG, F32)
    for r in range(NX):
        shard = chunk_of(r) * PER_X + lax.broadcasted_iota(
            jnp.int32, (NX * PER_X, CHUNK), 1
        ) // SLOTS
        expand = jnp.where(
            shard == lax.broadcasted_iota(jnp.int32, (NX * PER_X, CHUNK), 0), 1.0, 0.0
        )
        counts = dot(vc8, expand.astype(BF), 1, 0)[0:1]
        shard_row = chunk_of(r) * PER_X + lax.broadcasted_iota(jnp.int32, (1, CHUNK), 1) // SLOTS
        slot_row = (lax.broadcasted_iota(jnp.int32, (1, CHUNK), 1) % SLOTS).astype(F32)
        place = jnp.where(shard_row < c, -1.0, jnp.where(shard_row > c, 1e6, sel_keys))
        place = jnp.where(slot_row < counts, place, 1e6)
        scores = dot(queries, keys_of(r), 1, 1) * SCALE
        scores = jnp.where(place <= qpos_all, scores, NEG)
        s_ref[:, r * CHUNK:(r + 1) * CHUNK] = scores
        top = jnp.maximum(top, jnp.max(scores, axis=1, keepdims=True))
    norm = jnp.zeros((QROWS, 1), F32)
    for r in range(NX):
        terms = jnp.exp(s_ref[:, r * CHUNK:(r + 1) * CHUNK] - top)
        s_ref[:, r * CHUNK:(r + 1) * CHUNK] = terms
        norm = norm + jnp.sum(terms, axis=1, keepdims=True)
    inv = 1.0 / norm
    out = jnp.zeros((QROWS, HEAD), F32)
    for r in range(NX):
        probs = s_ref[:, r * CHUNK:(r + 1) * CHUNK] * inv
        s_ref[:, r * CHUNK:(r + 1) * CHUNK] = probs
        out = out + dot(probs.astype(BF), values_of(r), 1, 0)
    live_all = jnp.concatenate([live] * HEADS, axis=0)
    attended = (out * live_all).astype(BF)
    for h in range(HEADS):
        att_ref[:, h * HEAD:(h + 1) * HEAD] = attended[h * SLOTS:(h + 1) * SLOTS]
    out_dot = jnp.sum(grads.astype(F32) * attended.astype(F32), axis=1, keepdims=True)

    dq = jnp.zeros((QROWS, HEAD), F32)
    es, er = x_send.at[1], x_recv.at[1]
    for r in (2, 1, 3, 0):
        probs = s_ref[:, r * CHUNK:(r + 1) * CHUNK]
        grad_probs = dot(grads, values_of(r), 1, 1)
        ds = (probs * (grad_probs - out_dot) * SCALE).astype(BF)
        dq = dq + dot(ds, keys_of(r), 1, 0)
        kt = dot(ds, queries, 0, 0).reshape(NZ, NY, SLOTS, HEAD)
        vt = dot(probs.astype(BF), grads, 0, 0).reshape(NZ, NY, SLOTS, HEAD)
        if r == 2:
            tb[0, :, :, :, 0:HEAD] = kt.astype(BF)
            tb[0, :, :, :, HEAD:KV] = vt.astype(BF)
            send(tb.at[0, :, 0], hl, es.at[0], er.at[0], to_right)
            send(tb.at[0, :, 1], hr, es.at[1], er.at[1], to_left)
            continue
        tf[:, :, :, 0:HEAD] = kt
        tf[:, :, :, HEAD:KV] = vt
        if r == 1:
            arrived(hl, er.at[0], to_left)
            tf[:, 0] = tf[:, 0] + hl[...].astype(F32)
            tb[1] = tf[...].astype(BF)
            send(tb.at[1], cl, es.at[2], er.at[2], to_right)
        elif r == 3:
            arrived(hr, er.at[1], to_right)
            tf[:, 1] = tf[:, 1] + hr[...].astype(F32)
            tb[2] = tf[...].astype(BF)
            send(tb.at[2], cr, es.at[3], er.at[3], to_left)
    for h in range(HEADS):
        dq_ref[:, h * HEAD:(h + 1) * HEAD] = dq[h * SLOTS:(h + 1) * SLOTS].astype(BF)
    arrived(cl, er.at[2], to_left)
    arrived(cr, er.at[3], to_right)
    tf[...] = tf[...] + cl[...].astype(F32) + cr[...].astype(F32)
    ub[...] = tf[...].astype(BF)
    for d in ZORDER:
        send(ub.at[(z + d) % NZ], zr.at[z], z_send.at[4, d], z_recv.at[4, d], zpeer(d))
    total = tf[z]
    for d in ARRIVE:
        zs = (z + NZ - d) % NZ
        arrived(zr.at[zs], z_recv.at[4, d], zpeer(d))
        total = total + zr[zs].astype(F32)
    vs[...] = total
    send(vs.at[1 - y], yr, z_send.at[4, 0], z_recv.at[4, 0], to_y)
    arrived(yr, z_recv.at[4, 0], to_y)
    gz[z] = (vs[y] + yr[...]).astype(BF)

    for d in ZORDER:
        send(gz.at[z], gz.at[z], z_send.at[5, d], z_recv.at[5, d], zpeer(d))
    for d in ARRIVE:
        zs = (z + NZ - d) % NZ
        arrived(gz.at[zs], z_recv.at[5, d], zpeer(d))
    slot_grads = gz[...].reshape(NZ * SLOTS, KV)

    fs, fr = x_send.at[2], x_recv.at[2]
    ts, tsr = x_send.at[3], x_recv.at[3]

    def weight_part(r):
        return dot(xz[chunk_of(r)].reshape(NZ * SLOTS, KV), slot_grads, 0, 0).reshape(
            NY, HEAD, KV
        )

    def row_part(xx):
        return dot(slot_grads, wg[xx].reshape(NY * HEAD, KV), 1, 1)

    for k in range(2):
        rsb[k] = row_part(2 * k + 1 - core).astype(BF)
    send(rsb, rsr, ts.at[0], tsr.at[0], to_sib)
    wb[0] = weight_part(2).astype(BF)
    send(wb.at[0, 0], whl, fs.at[0], fr.at[0], to_right)
    send(wb.at[0, 1], whr, fs.at[1], fr.at[1], to_left)
    for k in range(2):
        rf[k] = row_part(2 * k + core)
    arrived(rsr, tsr.at[0], to_sib)
    ryb[...] = (rf[1 - ylo] + rsr[1 - ylo].astype(F32)).astype(BF)
    send(ryb, ryr, ts.at[1], tsr.at[1], to_ylo)
    wf[...] = weight_part(1)
    arrived(whl, fr.at[0], to_left)
    wf[0] = wf[0] + whl[...].astype(F32)
    wb[1] = wf[...].astype(BF)
    send(wb.at[1], wcl, fs.at[2], fr.at[2], to_right)
    wf[...] = weight_part(3)
    arrived(whr, fr.at[1], to_right)
    wf[1] = wf[1] + whr[...].astype(F32)
    wb[2] = wf[...].astype(BF)
    send(wb.at[2], wcr, fs.at[3], fr.at[3], to_left)
    arrived(ryr, tsr.at[1], to_ylo)
    tz[...] = (
        (rf[ylo] + rsr[ylo].astype(F32) + ryr[...].astype(F32)).astype(BF).reshape(NZ, SLOTS, KV)
    )
    for d in ZORDER:
        send(tz.at[(z + d) % NZ], tr.at[z], z_send.at[6, d], z_recv.at[6, d], zpeer(d))
    tr[z] = tz[z]
    wf[...] = weight_part(0)
    arrived(wcl, fr.at[2], to_left)
    arrived(wcr, fr.at[3], to_right)
    wf[...] = wf[...] + wcl[...].astype(F32) + wcr[...].astype(F32)
    wyb[...] = wf[1 - y].astype(BF)
    send(wyb, wyr, fs.at[4], fr.at[4], to_y)

    for d in ARRIVE:
        zs = (z + NZ - d) % NZ
        arrived(tr.at[zs], z_recv.at[6, d], zpeer(d))
    for zs in range(NZ):
        rows = (tr[zs].astype(F32) * live).astype(BF)
        tg_ref[:, zs * KV:(zs + 1) * KV] = dot(hot, rows, 0, 0).astype(BF)

    arrived(wyr, fr.at[4], to_y)
    both = (wf[y] + wyr[...].astype(F32)).astype(BF)
    kwg_ref[...] = both[:, 0:HEAD]
    vwg_ref[...] = both[:, HEAD:KV]

    for cp in started:
        cp.wait_send()


def local(tokens, select_index, valid_count, queries, key_matrix, value_matrix, out_grad):
    vmem = pl.BlockSpec(memory_space=pltpu.VMEM)
    dma = pltpu.SemaphoreType.DMA
    V = pltpu.VMEM
    shape = jax.ShapeDtypeStruct
    scratch = [
        V((ROWS, MODEL // 2), BF),
        V((NZ, 2, SLOTS, KV), BF),
        V((NX, NZ, SLOTS, KV), BF),
        V((NX, NY, HEAD, KV), BF),
        V((NZ, SLOTS, KV), F32),
        V((NZ, SLOTS, KV), F32),
        V((NX * PER_X, SLOTS, KV), BF),
        V((QROWS, NX * CHUNK), F32),
        V((QROWS, HEAD), BF),
        V((QROWS, HEAD), BF),
        V((NZ, NY, SLOTS, KV), F32),
        V((3, NZ, NY, SLOTS, KV), BF),
        V((NZ, SLOTS, KV), BF),
        V((NZ, SLOTS, KV), BF),
        V((NZ, NY, SLOTS, KV), BF),
        V((NZ, NY, SLOTS, KV), BF),
        V((NZ, NY, SLOTS, KV), BF),
        V((NZ, NY, SLOTS, KV), BF),
        V((NY, SLOTS, KV), F32),
        V((SLOTS, KV), F32),
        V((NZ, SLOTS, KV), BF),
        V((3, NY, HEAD, KV), BF),
        V((NY, HEAD, KV), F32),
        V((HEAD, KV), BF),
        V((HEAD, KV), BF),
        V((NY, HEAD, KV), BF),
        V((NY, HEAD, KV), BF),
        V((HEAD, KV), BF),
        V((HEAD, KV), BF),
        V((2, NZ * SLOTS, KV), BF),
        V((2, NZ * SLOTS, KV), BF),
        V((2, NZ * SLOTS, KV), F32),
        V((NZ * SLOTS, KV), BF),
        V((NZ * SLOTS, KV), BF),
        V((NZ, SLOTS, KV), BF),
        V((NZ, SLOTS, KV), BF),
        dma, dma((7, NZ)), dma((7, NZ)), dma((4, 8)), dma((4, 8)), dma((4, NZ)), dma((4, NZ)),
    ]
    att, dq, tg, kwg, vwg = pl.pallas_call(
        kernel,
        out_shape=(
            shape((SLOTS, HEADS * HEAD), BF),
            shape((SLOTS, HEADS * HEAD), BF),
            shape((ROWS, MODEL // 4), BF),
            shape((HEAD, HEAD), BF),
            shape((HEAD, HEAD), BF),
        ),
        in_specs=[pl.BlockSpec(memory_space=pl.ANY)] + [vmem] * 6,
        out_specs=(vmem,) * 5,
        scratch_shapes=scratch,
        compiler_params=pltpu.CompilerParams(
            collective_id=0, has_side_effects=True, vmem_limit_bytes=60 * 1024 * 1024
        ),
    )(
        tokens, select_index.reshape(1, -1), valid_count.reshape(1, -1), queries,
        key_matrix, value_matrix, out_grad,
    )
    return att, dq, tg, kwg, vwg


def solution(mesh):
    in_specs = (
        P("ctx", None), P("ctx"), P(), P("ctx", "tp"), P("ctx", "tp"), P("ctx", "tp"),
        P("ctx", "tp"),
    )
    out_specs = (P("ctx", "tp"),) * 5
    return jax.shard_map(local, mesh=mesh, in_specs=in_specs, out_specs=out_specs, check_vma=False)
```

```python
import math

import jax
import jax.numpy as jnp
from jax import lax
from jax.experimental import pallas as pl
from jax.experimental.pallas import tpu as pltpu
from jax.sharding import PartitionSpec as P

NX, NZ, NY = 4, 8, 2
HEAD = 128
SLOTS = 32
KV = 2 * HEAD
HEADS = 8
ROWS = 256
MODEL = 8192
PER_X = NZ * NY
CHUNK = PER_X * SLOTS
QROWS = HEADS * SLOTS
SCALE = 1.0 / math.sqrt(HEAD)
NEG = -1e30
BF = jnp.bfloat16
F32 = jnp.float32
ZORDER = (4, 3, 5, 2, 6, 1, 7)
ARRIVE = (1, 7, 2, 6, 3, 5, 4)
NEAREST = (0,) + ARRIVE
FARTHEST = ZORDER + (0,)
XORDER = ((2, 1), (2, 0), (1, 1), (3, 1), (1, 0), (3, 0), (0, 1))


def dot(a, b, ca, cb):
    return lax.dot_general(a, b, (((ca,), (cb,)), ((), ())), preferred_element_type=F32)


def kernel(
    tok_hbm, sel_hbm, vc_hbm, q_hbm, wk_hbm, wv_hbm, g_hbm,
    att_ref, dq_ref, rows_ref, wgr_ref,
    tok, sel_ref, vc_ref, q_ref, g_ref, pz, xz, wg, pf, pk, pv, rk, rv, kv, s_ref, qs, gs,
    tf, tf2, tb, hy, fb, fx, nl, nr, ub, zr, gz,
    wb, wf, wx, rsb, rsr, rf, ryb, ryr, tz, tr,
    in_sem, w_send, w_recv, z_send, z_recv, x_send, x_recv, ag_send, ag_recv, rs_send, rs_recv,
    t_send, t_recv,
):
    c = lax.axis_index("ctx")
    t = lax.axis_index("tp")
    x = c // PER_X
    z = (c // NY) % NZ
    y = c % NY
    core = t % 2
    ylo = t // 2
    right = (x + 1) % NX
    left = (x + NX - 1) % NX
    far = (x + 2) % NX

    def at(xx, zz, yy):
        return {"ctx": (xx * NZ + zz) * NY + yy, "tp": t}

    def zpeer(d):
        return at(x, (z + d) % NZ, y)

    def zpeer_y(d):
        return at(x, (z + d) % NZ, 1 - y)

    def half_of(k):
        return y if k == 0 else 1 - y

    def xpeer(r, k):
        return at((x + r) % NX, z, half_of(k))

    to_right = at(right, z, y)
    to_left = at(left, z, y)
    to_far = at(far, z, y)
    to_y = at(x, z, 1 - y)
    to_sib = {"ctx": c, "tp": 2 * ylo + 1 - core}
    to_ylo = {"ctx": c, "tp": 2 * (1 - ylo) + core}

    started = []

    def copy(src, dst, ssem, rsem, dev):
        return pltpu.make_async_remote_copy(
            src_ref=src, dst_ref=dst, send_sem=ssem, recv_sem=rsem,
            device_id=dev, device_id_type=pl.DeviceIdType.MESH,
        )

    def send(src, dst, ssem, rsem, dev):
        cp = copy(src, dst, ssem, rsem, dev)
        cp.start()
        started.append(cp)

    def arrived(dst, rsem, dev):
        copy(dst, dst, rsem, rsem, dev).wait_recv()

    barrier = pltpu.get_barrier_semaphore()
    partners = [zpeer(d) for d in range(1, NZ)] + [zpeer_y(d) for d in range(1, NZ)]
    partners += [xpeer(r, k) for r in range(1, NX) for k in range(2)] + [to_y, to_sib, to_ylo]
    for dev in partners:
        pl.semaphore_signal(barrier, inc=1, device_id=dev, device_id_type=pl.DeviceIdType.MESH)

    x_cols = NZ * KV
    loads = [pltpu.make_async_copy(sel_hbm, sel_ref, in_sem.at[0])]
    for k in range(2):
        c0 = pl.multiple_of((2 * core + k) * x_cols, x_cols)
        loads.append(
            pltpu.make_async_copy(tok_hbm.at[:, pl.ds(c0, x_cols)], tok.at[k], in_sem.at[1 + k])
        )
    loads.append(pltpu.make_async_copy(wk_hbm, wg.at[x, y, :, pl.ds(0, HEAD)], in_sem.at[3]))
    loads.append(pltpu.make_async_copy(wv_hbm, wg.at[x, y, :, pl.ds(HEAD, HEAD)], in_sem.at[4]))
    loads.append(pltpu.make_async_copy(vc_hbm, vc_ref, in_sem.at[5]))
    loads.append(pltpu.make_async_copy(q_hbm, q_ref, in_sem.at[6]))
    loads.append(pltpu.make_async_copy(g_hbm, g_ref, in_sem.at[7]))
    for cp in loads:
        cp.start()

    loads[0].wait()
    sel_row = jnp.broadcast_to(sel_ref[...], (SLOTS, SLOTS))
    i0 = lax.broadcasted_iota(jnp.int32, (SLOTS, SLOTS), 0)
    i1 = lax.broadcasted_iota(jnp.int32, (SLOTS, SLOTS), 1)
    sel_col = jnp.sum(jnp.where(i0 == i1, sel_row, 0), axis=1, keepdims=True)
    hot = jnp.where(
        lax.broadcasted_iota(jnp.int32, (SLOTS, ROWS), 1) == sel_col, 1.0, 0.0
    ).astype(BF)
    for k in range(2):
        loads[1 + k].wait()
        for zt in range(NZ):
            pz[zt, k] = dot(hot, tok[k, :, zt * KV:(zt + 1) * KV], 1, 0).astype(BF)
    xz[pl.ds(2 * core, 2), z] = pz[z]
    loads[3].wait()
    loads[4].wait()

    pl.semaphore_wait(barrier, len(partners))

    mine = wg.at[x, y]
    for r, k in XORDER:
        send(mine, mine, w_send.at[r, k], w_recv.at[r, k], xpeer(r, k))
    for d in ZORDER:
        send(
            pz.at[(z + d) % NZ], xz.at[pl.ds(2 * core, 2), z],
            z_send.at[0, d], z_recv.at[0, d], zpeer(d),
        )
    send(pz.at[z], xz.at[pl.ds(2 * core, 2), z], z_send.at[1, 0], z_recv.at[1, 0], to_sib)

    for cp in loads[5:]:
        cp.wait()
    vc = vc_ref[...]
    own_count = jnp.sum(
        jnp.where(lax.broadcasted_iota(jnp.int32, vc.shape, 1) == c, vc, 0), axis=1, keepdims=True
    )
    live_col = lax.broadcasted_iota(jnp.int32, (SLOTS, 1), 0) < own_count
    live = jnp.where(live_col, 1.0, 0.0)
    qpos = jnp.where(live_col, sel_col, ROWS).astype(F32)
    qpos_all = jnp.concatenate([qpos] * HEADS, axis=0)
    for h in range(HEADS):
        qs[h * SLOTS:(h + 1) * SLOTS, :] = q_ref[:, h * HEAD:(h + 1) * HEAD]
        gs[h * SLOTS:(h + 1) * SLOTS, :] = (
            g_ref[:, h * HEAD:(h + 1) * HEAD].astype(F32) * live
        ).astype(BF)

    def relay_picked(d):
        zs = (z + NZ - d) % NZ
        block = xz.at[pl.ds(2 * core, 2), zs]
        arrived(block, z_recv.at[0, d], zpeer(d))
        send(block, block, z_send.at[1, d], z_recv.at[1, d], to_sib)

    for d in ARRIVE:
        relay_picked(d)
    for r, k in XORDER:
        arrived(wg.at[(x + NX - r) % NX, half_of(k)], w_recv.at[r, k], xpeer(r, k))
    for d in NEAREST:
        zs = (z + NZ - d) % NZ
        arrived(xz.at[pl.ds(2 * (1 - core), 2), zs], z_recv.at[1, d], to_sib)

    acc = jnp.zeros((NZ * SLOTS, KV), F32)
    for xx in range(NX):
        acc = acc + dot(
            xz[xx].reshape(NZ * SLOTS, KV), wg[xx].reshape(NY * HEAD, KV), 1, 0
        )
    pf[...] = acc.reshape(NZ, SLOTS, KV)
    pk[...] = pf[:, :, 0:HEAD]
    pv[...] = pf[:, :, HEAD:KV].astype(BF)
    for d in ZORDER:
        zt = (z + d) % NZ
        send(pk.at[zt], rk.at[z], z_send.at[2, d], z_recv.at[2, d], zpeer(d))
        send(pv.at[zt], rv.at[z], t_send.at[4, d], t_recv.at[4, d], zpeer(d))
    key_sum = pf[z, :, 0:HEAD]
    value_sum = pf[z, :, HEAD:KV]
    for d in ARRIVE:
        zs = (z + NZ - d) % NZ
        arrived(rk.at[zs], z_recv.at[2, d], zpeer(d))
        key_sum = key_sum + rk[zs]
        arrived(rv.at[zs], t_recv.at[4, d], zpeer(d))
        value_sum = value_sum + rv[zs].astype(F32)
    kv[c, :, 0:HEAD] = key_sum.astype(BF)
    kv[c, :, HEAD:KV] = value_sum.astype(BF)

    def one(xx, zz, yy):
        return kv.at[(xx * NZ + zz) * NY + yy]

    def spread_near(block, d, k):
        send(block, block, ag_send.at[k, d], ag_recv.at[k, d], to_right)
        send(block, block, ag_send.at[k + 1, d], ag_recv.at[k + 1, d], to_left)

    def own_block(d):
        block = one(x, (z + NZ - d) % NZ, y)
        if d:
            arrived(block, z_recv.at[3, d], zpeer(d))
        send(block, block, ag_send.at[4, d], ag_recv.at[4, d], to_far)
        spread_near(block, d, 0)

    def peer_block(d):
        block = one(x, (z + NZ - d) % NZ, 1 - y)
        arrived(block, z_recv.at[6, d], zpeer_y(d))
        spread_near(block, d, 2)

    def far_block(d):
        block = one(far, (z + NZ - d) % NZ, y)
        arrived(block, ag_recv.at[4, d], to_far)
        send(block, block, ag_send.at[5, d], ag_recv.at[5, d], to_y)

    own = one(x, z, y)
    for d in ZORDER:
        send(own, own, z_send.at[3, d], z_recv.at[3, d], zpeer(d))
    own_block(0)
    for d in FARTHEST:
        send(own, own, z_send.at[6, d], z_recv.at[6, d], zpeer_y(d))
    for d in ARRIVE:
        own_block(d)
    peer_block(0)
    far_block(0)
    for d in ARRIVE:
        peer_block(d)
        far_block(d)
    for d in NEAREST:
        zs = (z + NZ - d) % NZ
        arrived(one(left, zs, y), ag_recv.at[0, d], to_left)
        arrived(one(right, zs, y), ag_recv.at[1, d], to_right)
        arrived(one(left, zs, 1 - y), ag_recv.at[2, d], to_left)
        arrived(one(right, zs, 1 - y), ag_recv.at[3, d], to_right)
    for d in NEAREST:
        arrived(one(far, (z + NZ - d) % NZ, 1 - y), ag_recv.at[5, d], to_y)

    vc8 = jnp.broadcast_to(vc.astype(F32), (8, NX * PER_X)).astype(BF)
    sel8 = jnp.broadcast_to(sel_ref[...].astype(F32), (8, SLOTS)).astype(BF)
    jslot = lax.broadcasted_iota(jnp.int32, (SLOTS, CHUNK), 1) % SLOTS
    spread = jnp.where(jslot == lax.broadcasted_iota(jnp.int32, (SLOTS, CHUNK), 0), 1.0, 0.0)
    sel_keys = dot(sel8, spread.astype(BF), 1, 0)[0:1]
    queries = qs[...]
    grads = gs[...]

    def chunk_of(r):
        return (x + r) % NX

    def keys_of(r):
        return kv[pl.ds(chunk_of(r) * PER_X, PER_X), :, 0:HEAD].reshape(CHUNK, HEAD)

    def values_of(r):
        return kv[pl.ds(chunk_of(r) * PER_X, PER_X), :, HEAD:KV].reshape(CHUNK, HEAD)

    top = jnp.full((QROWS, 1), NEG, F32)
    for r in range(NX):
        shard = chunk_of(r) * PER_X + lax.broadcasted_iota(
            jnp.int32, (NX * PER_X, CHUNK), 1
        ) // SLOTS
        expand = jnp.where(
            shard == lax.broadcasted_iota(jnp.int32, (NX * PER_X, CHUNK), 0), 1.0, 0.0
        )
        counts = dot(vc8, expand.astype(BF), 1, 0)[0:1]
        shard_row = chunk_of(r) * PER_X + lax.broadcasted_iota(jnp.int32, (1, CHUNK), 1) // SLOTS
        slot_row = (lax.broadcasted_iota(jnp.int32, (1, CHUNK), 1) % SLOTS).astype(F32)
        place = jnp.where(shard_row < c, -1.0, jnp.where(shard_row > c, 1e6, sel_keys))
        place = jnp.where(slot_row < counts, place, 1e6)
        scores = dot(queries, keys_of(r), 1, 1) * SCALE
        scores = jnp.where(place <= qpos_all, scores, NEG)
        s_ref[:, r * CHUNK:(r + 1) * CHUNK] = scores
        top = jnp.maximum(top, jnp.max(scores, axis=1, keepdims=True))
    norm = jnp.zeros((QROWS, 1), F32)
    for r in range(NX):
        terms = jnp.exp(s_ref[:, r * CHUNK:(r + 1) * CHUNK] - top)
        s_ref[:, r * CHUNK:(r + 1) * CHUNK] = terms
        norm = norm + jnp.sum(terms, axis=1, keepdims=True)
    inv = 1.0 / norm
    out = jnp.zeros((QROWS, HEAD), F32)
    for r in range(NX):
        probs = s_ref[:, r * CHUNK:(r + 1) * CHUNK] * inv
        s_ref[:, r * CHUNK:(r + 1) * CHUNK] = probs
        out = out + dot(probs.astype(BF), values_of(r), 1, 0)
    live_all = jnp.concatenate([live] * HEADS, axis=0)
    attended = (out * live_all).astype(BF)
    for h in range(HEADS):
        att_ref[:, h * HEAD:(h + 1) * HEAD] = attended[h * SLOTS:(h + 1) * SLOTS]
    out_dot = jnp.sum(grads.astype(F32) * attended.astype(F32), axis=1, keepdims=True)

    dq = jnp.zeros((QROWS, HEAD), F32)

    def column(r, dq):
        probs = s_ref[:, r * CHUNK:(r + 1) * CHUNK]
        grad_probs = dot(grads, values_of(r), 1, 1)
        ds = (probs * (grad_probs - out_dot) * SCALE).astype(BF)
        dq = dq + dot(ds, keys_of(r), 1, 0)
        kt = dot(ds, queries, 0, 0).reshape(NZ, NY, SLOTS, HEAD)
        vt = dot(probs.astype(BF), grads, 0, 0).reshape(NZ, NY, SLOTS, HEAD)
        return dq, kt, vt

    dq, kt, vt = column(2, dq)
    tf2[:, :, :, 0:HEAD] = kt
    tf2[:, :, :, HEAD:KV] = vt
    tb[0] = tf2[...].astype(BF)
    for d in FARTHEST:
        zt = (z + d) % NZ
        send(tb.at[0, zt, 1 - y], hy.at[zt], rs_send.at[0, d], rs_recv.at[0, d], to_y)
    for k, r in ((1, 1), (2, 3)):
        dq, kt, vt = column(r, dq)
        tb[k, :, :, :, 0:HEAD] = kt.astype(BF)
        tb[k, :, :, :, HEAD:KV] = vt.astype(BF)

    def near(d):
        zt = (z + d) % NZ
        send(tb.at[1, zt], nl.at[zt], rs_send.at[1, d], rs_recv.at[1, d], to_right)
        send(tb.at[2, zt], nr.at[zt], rs_send.at[2, d], rs_recv.at[2, d], to_left)

    def distant(d):
        zt = (z + d) % NZ
        arrived(hy.at[zt], rs_recv.at[0, d], to_y)
        fb[zt] = (tf2[zt, y] + hy[zt].astype(F32)).astype(BF)
        send(fb.at[zt], fx.at[zt], rs_send.at[3, d], rs_recv.at[3, d], to_far)

    for d in FARTHEST[:3]:
        near(d)
    dq, kt, vt = column(0, dq)
    tf[:, :, :, 0:HEAD] = kt
    tf[:, :, :, HEAD:KV] = vt
    for d in FARTHEST[:3]:
        distant(d)
    for d in FARTHEST[3:]:
        near(d)
        distant(d)
    for h in range(HEADS):
        dq_ref[:, h * HEAD:(h + 1) * HEAD] = dq[h * SLOTS:(h + 1) * SLOTS].astype(BF)
    for d in FARTHEST:
        zt = (z + d) % NZ
        arrived(nl.at[zt], rs_recv.at[1, d], to_left)
        arrived(nr.at[zt], rs_recv.at[2, d], to_right)
        tf[zt] = tf[zt] + nl[zt].astype(F32) + nr[zt].astype(F32)
        arrived(fx.at[zt], rs_recv.at[3, d], to_far)
        tf[zt, y] = tf[zt, y] + fx[zt].astype(F32)
        ub[zt] = tf[zt].astype(BF)
        if d:
            send(ub.at[zt, y], zr.at[z, y], z_send.at[4, d], z_recv.at[4, d], zpeer(d))
        send(ub.at[zt, 1 - y], zr.at[z, y], t_send.at[0, d], t_recv.at[0, d], zpeer_y(d))
    total = tf[z, y]
    arrived(zr.at[z, 1 - y], t_recv.at[0, 0], to_y)
    total = total + zr[z, 1 - y].astype(F32)
    for d in ARRIVE:
        zs = (z + NZ - d) % NZ
        arrived(zr.at[zs, y], z_recv.at[4, d], zpeer(d))
        arrived(zr.at[zs, 1 - y], t_recv.at[0, d], zpeer_y(d))
        total = total + zr[zs, y].astype(F32) + zr[zs, 1 - y].astype(F32)
    gz[z] = total.astype(BF)

    for d in ZORDER:
        send(gz.at[z], gz.at[z], z_send.at[5, d], z_recv.at[5, d], zpeer(d))
    for d in ARRIVE:
        zs = (z + NZ - d) % NZ
        arrived(gz.at[zs], z_recv.at[5, d], zpeer(d))
    slot_grads = gz[...].reshape(NZ * SLOTS, KV)


    def weight_part(r):
        return dot(xz[chunk_of(r)].reshape(NZ * SLOTS, KV), slot_grads, 0, 0).reshape(
            NY, HEAD, KV
        )

    def row_part(xx):
        return dot(slot_grads, wg[xx].reshape(NY * HEAD, KV), 1, 1).reshape(NZ, SLOTS, KV)

    for k in range(2):
        rsb[:, k] = row_part(2 * k + 1 - core).astype(BF)
    for d in FARTHEST:
        zt = (z + d) % NZ
        send(rsb.at[zt], rsr.at[zt], t_send.at[1, d], t_recv.at[1, d], to_sib)
    for r in (2, 1, 3):
        wb[r] = weight_part(r).astype(BF)
        for k in (1, 0):
            send(wb.at[r, half_of(k)], wx.at[r, k], x_send.at[r, k], x_recv.at[r, k], xpeer(r, k))
    for k in range(2):
        rf[:, k] = row_part(2 * k + core)
    for d in FARTHEST:
        zt = (z + d) % NZ
        arrived(rsr.at[zt], t_recv.at[1, d], to_sib)
        ryb[zt] = (rf[zt, 1 - ylo] + rsr[zt, 1 - ylo].astype(F32)).astype(BF)
        send(ryb.at[zt], ryr.at[zt], t_send.at[2, d], t_recv.at[2, d], to_ylo)
    wf[...] = weight_part(0)
    wb[0] = wf[...].astype(BF)
    send(wb.at[0, 1 - y], wx.at[0, 1], x_send.at[0, 1], x_recv.at[0, 1], to_y)
    for d in FARTHEST:
        zt = (z + d) % NZ
        arrived(ryr.at[zt], t_recv.at[2, d], to_ylo)
        tz[zt] = (
            rf[zt, ylo] + rsr[zt, ylo].astype(F32) + ryr[zt].astype(F32)
        ).astype(BF)
        if d:
            send(tz.at[zt], tr.at[z], t_send.at[3, d], t_recv.at[3, d], zpeer(d))
    tr[z] = tz[z]
    for d in ARRIVE:
        zs = (z + NZ - d) % NZ
        arrived(tr.at[zs], t_recv.at[3, d], zpeer(d))
    for zs in range(NZ):
        rows_ref[:, zs * KV:(zs + 1) * KV] = (tr[zs].astype(F32) * live).astype(BF)

    total = wf[y]
    for r, k in XORDER:
        arrived(wx.at[r, k], x_recv.at[r, k], xpeer(NX - r, k))
        total = total + wx[r, k].astype(F32)
    wgr_ref[...] = total.astype(BF)

    for cp in started:
        cp.wait_send()


def finish(
    sel_ref, att_in, dq_in, rows_ref, wgr_ref, att_ref, dq_ref, tg_ref, kwg_ref, vwg_ref
):
    sel_row = jnp.broadcast_to(sel_ref[...], (ROWS, SLOTS))
    place = jnp.where(
        lax.broadcasted_iota(jnp.int32, (ROWS, SLOTS), 0) == sel_row, 1.0, 0.0
    ).astype(BF)
    for k in range(NZ):
        tg_ref[:, k * KV:(k + 1) * KV] = dot(
            place, rows_ref[:, k * KV:(k + 1) * KV], 1, 0
        ).astype(BF)
    att_ref[...] = att_in[...]
    dq_ref[...] = dq_in[...]
    kwg_ref[...] = wgr_ref[:, 0:HEAD]
    vwg_ref[...] = wgr_ref[:, HEAD:KV]


def local(tokens, select_index, valid_count, queries, key_matrix, value_matrix, out_grad):
    vmem = pl.BlockSpec(memory_space=pltpu.VMEM)
    dma = pltpu.SemaphoreType.DMA
    V = pltpu.VMEM
    shape = jax.ShapeDtypeStruct
    block = (NZ, SLOTS, KV)
    pairs = (NZ, NY, SLOTS, KV)
    scratch = [
        V((2, ROWS, NZ * KV), BF),
        V((1, SLOTS), jnp.int32),
        V((1, NX * PER_X), jnp.int32),
        V((SLOTS, HEADS * HEAD), BF),
        V((SLOTS, HEADS * HEAD), BF),
        V((NZ, 2, SLOTS, KV), BF),
        V((NX, NZ, SLOTS, KV), BF),
        V((NX, NY, HEAD, KV), BF),
        V(block, F32),
        V((NZ, SLOTS, HEAD), F32),
        V((NZ, SLOTS, HEAD), BF),
        V((NZ, SLOTS, HEAD), F32),
        V((NZ, SLOTS, HEAD), BF),
        V((NX * PER_X, SLOTS, KV), BF),
        V((QROWS, NX * CHUNK), F32),
        V((QROWS, HEAD), BF),
        V((QROWS, HEAD), BF),
        V(pairs, F32),
        V(pairs, F32),
        V((3,) + pairs, BF),
        V(block, BF),
        V(block, BF),
        V(block, BF),
        V(pairs, BF),
        V(pairs, BF),
        V(pairs, BF),
        V(pairs, BF),
        V(block, BF),
        V((NX, NY, HEAD, KV), BF),
        V((NY, HEAD, KV), F32),
        V((NX, 2, HEAD, KV), BF),
        V((NZ, 2, SLOTS, KV), BF),
        V((NZ, 2, SLOTS, KV), BF),
        V((NZ, 2, SLOTS, KV), F32),
        V(block, BF),
        V(block, BF),
        V(block, BF),
        V(block, BF),
        dma((8,)), dma((NX, 2)), dma((NX, 2)), dma((7, NZ)), dma((7, NZ)), dma((NX, 2)),
        dma((NX, 2)),
        dma((6, NZ)), dma((6, NZ)), dma((4, NZ)), dma((4, NZ)), dma((5, NZ)), dma((5, NZ)),
    ]
    sel = select_index.reshape(1, -1)
    att, dq, rows, wgr = pl.pallas_call(
        kernel,
        out_shape=(
            shape((SLOTS, HEADS * HEAD), BF),
            shape((SLOTS, HEADS * HEAD), BF),
            shape((SLOTS, MODEL // 4), BF),
            shape((HEAD, KV), BF),
        ),
        in_specs=[pl.BlockSpec(memory_space=pl.ANY)] * 7,
        out_specs=(vmem,) * 4,
        scratch_shapes=scratch,
        compiler_params=pltpu.CompilerParams(
            collective_id=0, has_side_effects=True, vmem_limit_bytes=62 * 1024 * 1024
        ),
    )(tokens, sel, valid_count.reshape(1, -1), queries, key_matrix, value_matrix, out_grad)
    return pl.pallas_call(
        finish,
        out_shape=(
            shape((SLOTS, HEADS * HEAD), BF),
            shape((SLOTS, HEADS * HEAD), BF),
            shape((ROWS, MODEL // 4), BF),
            shape((HEAD, HEAD), BF),
            shape((HEAD, HEAD), BF),
        ),
        in_specs=[vmem] * 5,
        out_specs=(vmem,) * 5,
        compiler_params=pltpu.CompilerParams(vmem_limit_bytes=6 * 1024 * 1024),
    )(sel, att, dq, rows, wgr)


def solution(mesh):
    in_specs = (
        P("ctx", None), P("ctx"), P(), P("ctx", "tp"), P("ctx", "tp"), P("ctx", "tp"),
        P("ctx", "tp"),
    )
    out_specs = (P("ctx", "tp"),) * 5
    return jax.shard_map(local, mesh=mesh, in_specs=in_specs, out_specs=out_specs, check_vma=False)
```

```python
import math

import jax
import jax.numpy as jnp
from jax import lax
from jax.experimental import pallas as pl
from jax.experimental.pallas import tpu as pltpu
from jax.sharding import PartitionSpec as P

NX, NZ, NY = 4, 8, 2
HEAD = 128
SLOTS = 32
KV = 2 * HEAD
HEADS = 8
ROWS = 256
MODEL = 8192
PER_X = NZ * NY
CHUNK = PER_X * SLOTS
QROWS = HEADS * SLOTS
SCALE = 1.0 / math.sqrt(HEAD)
NEG = -1e30
BF = jnp.bfloat16
F32 = jnp.float32
ZORDER = (4, 3, 5, 2, 6, 1, 7)
ARRIVE = (1, 7, 2, 6, 3, 5, 4)
NEAREST = (0,) + ARRIVE
FARTHEST = ZORDER + (0,)
XORDER = ((2, 1), (2, 0), (1, 1), (3, 1), (1, 0), (3, 0), (0, 1))


def dot(a, b, ca, cb):
    return lax.dot_general(a, b, (((ca,), (cb,)), ((), ())), preferred_element_type=F32)


def kernel(
    tok_hbm, sel_hbm, vc_hbm, q_hbm, wk_hbm, wv_hbm, g_hbm,
    att_ref, dq_ref, rows_ref, wgr_ref,
    tok, sel_ref, vc_ref, q_ref, g_ref, pz, xz, wg, pf, pk, pv, rk, rv, kv, s_ref, qs, gs,
    tf, tf2, tb, hy, fb, fx, nl, nr, ub, zr, gz,
    wb, wf, wx, rsb, rsr, rf, ryb, ryr, tz, tr,
    in_sem, w_send, w_recv, z_send, z_recv, x_send, x_recv, ag_send, ag_recv, rs_send, rs_recv,
    t_send, t_recv,
):
    c = lax.axis_index("ctx")
    t = lax.axis_index("tp")
    x = c // PER_X
    z = (c // NY) % NZ
    y = c % NY
    core = t % 2
    ylo = t // 2
    right = (x + 1) % NX
    left = (x + NX - 1) % NX
    far = (x + 2) % NX

    def at(xx, zz, yy):
        return {"ctx": (xx * NZ + zz) * NY + yy, "tp": t}

    def zpeer(d):
        return at(x, (z + d) % NZ, y)

    def zpeer_y(d):
        return at(x, (z + d) % NZ, 1 - y)

    def half_of(k):
        return y if k == 0 else 1 - y

    def xpeer(r, k):
        return at((x + r) % NX, z, half_of(k))

    to_right = at(right, z, y)
    to_left = at(left, z, y)
    to_far = at(far, z, y)
    to_y = at(x, z, 1 - y)
    to_sib = {"ctx": c, "tp": 2 * ylo + 1 - core}
    to_ylo = {"ctx": c, "tp": 2 * (1 - ylo) + core}

    started = []

    def copy(src, dst, ssem, rsem, dev):
        return pltpu.make_async_remote_copy(
            src_ref=src, dst_ref=dst, send_sem=ssem, recv_sem=rsem,
            device_id=dev, device_id_type=pl.DeviceIdType.MESH,
        )

    def send(src, dst, ssem, rsem, dev):
        cp = copy(src, dst, ssem, rsem, dev)
        cp.start()
        started.append(cp)

    def arrived(dst, rsem, dev):
        copy(dst, dst, rsem, rsem, dev).wait_recv()

    barrier = pltpu.get_barrier_semaphore()
    partners = [zpeer(d) for d in range(1, NZ)] + [zpeer_y(d) for d in range(1, NZ)]
    partners += [xpeer(r, k) for r in range(1, NX) for k in range(2)] + [to_y, to_sib, to_ylo]
    for dev in partners:
        pl.semaphore_signal(barrier, inc=1, device_id=dev, device_id_type=pl.DeviceIdType.MESH)

    x_cols = NZ * KV
    loads = [pltpu.make_async_copy(sel_hbm, sel_ref, in_sem.at[0])]
    for k in range(2):
        c0 = pl.multiple_of((2 * core + k) * x_cols, x_cols)
        loads.append(
            pltpu.make_async_copy(tok_hbm.at[:, pl.ds(c0, x_cols)], tok.at[k], in_sem.at[1 + k])
        )
    loads.append(pltpu.make_async_copy(wk_hbm, wg.at[x, y, :, pl.ds(0, HEAD)], in_sem.at[3]))
    loads.append(pltpu.make_async_copy(wv_hbm, wg.at[x, y, :, pl.ds(HEAD, HEAD)], in_sem.at[4]))
    loads.append(pltpu.make_async_copy(vc_hbm, vc_ref, in_sem.at[5]))
    loads.append(pltpu.make_async_copy(q_hbm, q_ref, in_sem.at[6]))
    loads.append(pltpu.make_async_copy(g_hbm, g_ref, in_sem.at[7]))
    for cp in loads:
        cp.start()

    loads[0].wait()
    sel_row = jnp.broadcast_to(sel_ref[...], (SLOTS, SLOTS))
    i0 = lax.broadcasted_iota(jnp.int32, (SLOTS, SLOTS), 0)
    i1 = lax.broadcasted_iota(jnp.int32, (SLOTS, SLOTS), 1)
    sel_col = jnp.sum(jnp.where(i0 == i1, sel_row, 0), axis=1, keepdims=True)
    hot = jnp.where(
        lax.broadcasted_iota(jnp.int32, (SLOTS, ROWS), 1) == sel_col, 1.0, 0.0
    ).astype(BF)
    for k in range(2):
        loads[1 + k].wait()
        for zt in range(NZ):
            pz[zt, k] = dot(hot, tok[k, :, zt * KV:(zt + 1) * KV], 1, 0).astype(BF)
    xz[pl.ds(2 * core, 2), z] = pz[z]
    loads[3].wait()
    loads[4].wait()

    pl.semaphore_wait(barrier, len(partners))

    mine = wg.at[x, y]
    for r, k in XORDER:
        send(mine, mine, w_send.at[r, k], w_recv.at[r, k], xpeer(r, k))
    for d in ZORDER:
        send(
            pz.at[(z + d) % NZ], xz.at[pl.ds(2 * core, 2), z],
            z_send.at[0, d], z_recv.at[0, d], zpeer(d),
        )
    send(pz.at[z], xz.at[pl.ds(2 * core, 2), z], z_send.at[1, 0], z_recv.at[1, 0], to_sib)

    for cp in loads[5:]:
        cp.wait()
    vc = vc_ref[...]
    own_count = jnp.sum(
        jnp.where(lax.broadcasted_iota(jnp.int32, vc.shape, 1) == c, vc, 0), axis=1, keepdims=True
    )
    live_col = lax.broadcasted_iota(jnp.int32, (SLOTS, 1), 0) < own_count
    live = jnp.where(live_col, 1.0, 0.0)
    qpos = jnp.where(live_col, sel_col, ROWS).astype(F32)
    qpos_all = jnp.concatenate([qpos] * HEADS, axis=0)
    for h in range(HEADS):
        qs[h * SLOTS:(h + 1) * SLOTS, :] = q_ref[:, h * HEAD:(h + 1) * HEAD]
        gs[h * SLOTS:(h + 1) * SLOTS, :] = (
            g_ref[:, h * HEAD:(h + 1) * HEAD].astype(F32) * live
        ).astype(BF)

    def relay_picked(d):
        zs = (z + NZ - d) % NZ
        block = xz.at[pl.ds(2 * core, 2), zs]
        arrived(block, z_recv.at[0, d], zpeer(d))
        send(block, block, z_send.at[1, d], z_recv.at[1, d], to_sib)

    for d in ARRIVE:
        relay_picked(d)
    for r, k in XORDER:
        arrived(wg.at[(x + NX - r) % NX, half_of(k)], w_recv.at[r, k], xpeer(r, k))
    for d in NEAREST:
        zs = (z + NZ - d) % NZ
        arrived(xz.at[pl.ds(2 * (1 - core), 2), zs], z_recv.at[1, d], to_sib)

    acc = jnp.zeros((NZ * SLOTS, KV), F32)
    for xx in range(NX):
        acc = acc + dot(
            xz[xx].reshape(NZ * SLOTS, KV), wg[xx].reshape(NY * HEAD, KV), 1, 0
        )
    pf[...] = acc.reshape(NZ, SLOTS, KV)
    pk[...] = pf[:, :, 0:HEAD]
    pv[...] = pf[:, :, HEAD:KV].astype(BF)
    for d in ZORDER:
        zt = (z + d) % NZ
        send(pk.at[zt], rk.at[z], z_send.at[2, d], z_recv.at[2, d], zpeer(d))
        send(pv.at[zt], rv.at[z], t_send.at[4, d], t_recv.at[4, d], zpeer(d))
    key_sum = pf[z, :, 0:HEAD]
    value_sum = pf[z, :, HEAD:KV]
    for d in ARRIVE:
        zs = (z + NZ - d) % NZ
        arrived(rk.at[zs], z_recv.at[2, d], zpeer(d))
        key_sum = key_sum + rk[zs]
        arrived(rv.at[zs], t_recv.at[4, d], zpeer(d))
        value_sum = value_sum + rv[zs].astype(F32)
    kv[c, :, 0:HEAD] = key_sum.astype(BF)
    kv[c, :, HEAD:KV] = value_sum.astype(BF)

    def one(xx, zz, yy):
        return kv.at[(xx * NZ + zz) * NY + yy]

    def spread_near(block, d, k):
        send(block, block, ag_send.at[k, d], ag_recv.at[k, d], to_right)
        send(block, block, ag_send.at[k + 1, d], ag_recv.at[k + 1, d], to_left)

    def own_block(d):
        block = one(x, (z + NZ - d) % NZ, y)
        if d:
            arrived(block, z_recv.at[3, d], zpeer(d))
        if d == 4:
            send(block, block, ag_send.at[5, d], ag_recv.at[5, d], xpeer(2, 1))
        send(block, block, ag_send.at[4, d], ag_recv.at[4, d], to_far)
        spread_near(block, d, 0)

    def peer_block(d):
        block = one(x, (z + NZ - d) % NZ, 1 - y)
        arrived(block, z_recv.at[6, d], zpeer_y(d))
        spread_near(block, d, 2)

    def far_block(d):
        block = one(far, (z + NZ - d) % NZ, y)
        arrived(block, ag_recv.at[4, d], to_far)
        if d != 4:
            send(block, block, ag_send.at[5, d], ag_recv.at[5, d], to_y)

    own = one(x, z, y)
    send(own, own, z_send.at[6, 0], z_recv.at[6, 0], to_y)
    for d in ARRIVE:
        send(own, own, z_send.at[3, d], z_recv.at[3, d], zpeer(d))
    own_block(0)
    for d in ARRIVE:
        send(own, own, z_send.at[6, d], z_recv.at[6, d], zpeer_y(d))
    own_block(1)
    own_block(7)
    peer_block(0)
    own_block(2)
    own_block(6)
    far_block(0)
    own_block(3)
    own_block(5)
    peer_block(1)
    peer_block(7)
    own_block(4)
    far_block(1)
    far_block(7)
    peer_block(2)
    peer_block(6)
    far_block(2)
    far_block(6)
    peer_block(3)
    peer_block(5)
    far_block(3)
    far_block(5)
    peer_block(4)
    far_block(4)

    vc8 = jnp.broadcast_to(vc.astype(F32), (8, NX * PER_X)).astype(BF)
    sel8 = jnp.broadcast_to(sel_ref[...].astype(F32), (8, SLOTS)).astype(BF)
    jslot = lax.broadcasted_iota(jnp.int32, (SLOTS, CHUNK), 1) % SLOTS
    spread = jnp.where(jslot == lax.broadcasted_iota(jnp.int32, (SLOTS, CHUNK), 0), 1.0, 0.0)
    sel_keys = dot(sel8, spread.astype(BF), 1, 0)[0:1]
    queries = qs[...]
    grads = gs[...]

    def chunk_of(r):
        return (x + r) % NX

    def keys_of(r):
        return kv[pl.ds(chunk_of(r) * PER_X, PER_X), :, 0:HEAD].reshape(CHUNK, HEAD)

    def values_of(r):
        return kv[pl.ds(chunk_of(r) * PER_X, PER_X), :, HEAD:KV].reshape(CHUNK, HEAD)

    def score(r):
        shard = chunk_of(r) * PER_X + lax.broadcasted_iota(
            jnp.int32, (NX * PER_X, CHUNK), 1
        ) // SLOTS
        expand = jnp.where(
            shard == lax.broadcasted_iota(jnp.int32, (NX * PER_X, CHUNK), 0), 1.0, 0.0
        )
        counts = dot(vc8, expand.astype(BF), 1, 0)[0:1]
        shard_row = chunk_of(r) * PER_X + lax.broadcasted_iota(jnp.int32, (1, CHUNK), 1) // SLOTS
        slot_row = (lax.broadcasted_iota(jnp.int32, (1, CHUNK), 1) % SLOTS).astype(F32)
        place = jnp.where(shard_row < c, -1.0, jnp.where(shard_row > c, 1e6, sel_keys))
        place = jnp.where(slot_row < counts, place, 1e6)
        scores = dot(queries, keys_of(r), 1, 1) * SCALE
        scores = jnp.where(place <= qpos_all, scores, NEG)
        s_ref[:, r * CHUNK:(r + 1) * CHUNK] = scores
        return jnp.max(scores, axis=1, keepdims=True)

    top = score(0)
    for d in NEAREST:
        zs = (z + NZ - d) % NZ
        arrived(one(left, zs, y), ag_recv.at[0, d], to_left)
        arrived(one(right, zs, y), ag_recv.at[1, d], to_right)
        arrived(one(left, zs, 1 - y), ag_recv.at[2, d], to_left)
        arrived(one(right, zs, 1 - y), ag_recv.at[3, d], to_right)
    top = jnp.maximum(top, score(1))
    top = jnp.maximum(top, score(3))
    for d in NEAREST:
        arrived(one(far, (z + NZ - d) % NZ, 1 - y), ag_recv.at[5, d], xpeer(2, 1))
    top = jnp.maximum(top, score(2))
    norm = jnp.zeros((QROWS, 1), F32)
    for r in range(NX):
        terms = jnp.exp(s_ref[:, r * CHUNK:(r + 1) * CHUNK] - top)
        s_ref[:, r * CHUNK:(r + 1) * CHUNK] = terms
        norm = norm + jnp.sum(terms, axis=1, keepdims=True)
    inv = 1.0 / norm
    out = jnp.zeros((QROWS, HEAD), F32)
    for r in range(NX):
        probs = s_ref[:, r * CHUNK:(r + 1) * CHUNK] * inv
        s_ref[:, r * CHUNK:(r + 1) * CHUNK] = probs
        out = out + dot(probs.astype(BF), values_of(r), 1, 0)
    live_all = jnp.concatenate([live] * HEADS, axis=0)
    attended = (out * live_all).astype(BF)
    for h in range(HEADS):
        att_ref[:, h * HEAD:(h + 1) * HEAD] = attended[h * SLOTS:(h + 1) * SLOTS]
    out_dot = jnp.sum(grads.astype(F32) * attended.astype(F32), axis=1, keepdims=True)

    dq = jnp.zeros((QROWS, HEAD), F32)

    def column(r, dq):
        probs = s_ref[:, r * CHUNK:(r + 1) * CHUNK]
        grad_probs = dot(grads, values_of(r), 1, 1)
        ds = (probs * (grad_probs - out_dot) * SCALE).astype(BF)
        dq = dq + dot(ds, keys_of(r), 1, 0)
        kt = dot(ds, queries, 0, 0).reshape(NZ, NY, SLOTS, HEAD)
        vt = dot(probs.astype(BF), grads, 0, 0).reshape(NZ, NY, SLOTS, HEAD)
        return dq, kt, vt

    dq, kt, vt = column(2, dq)
    tf2[:, :, :, 0:HEAD] = kt
    tf2[:, :, :, HEAD:KV] = vt
    tb[0] = tf2[...].astype(BF)
    for d in FARTHEST:
        zt = (z + d) % NZ
        send(tb.at[0, zt, 1 - y], hy.at[zt], rs_send.at[0, d], rs_recv.at[0, d], to_y)
    def near(d, k):
        zt = (z + d) % NZ
        if k == 1:
            send(tb.at[1, zt], nl.at[zt], rs_send.at[1, d], rs_recv.at[1, d], to_right)
        else:
            send(tb.at[2, zt], nr.at[zt], rs_send.at[2, d], rs_recv.at[2, d], to_left)

    for k, r in ((1, 1), (2, 3)):
        dq, kt, vt = column(r, dq)
        tb[k, :, :, :, 0:HEAD] = kt.astype(BF)
        tb[k, :, :, :, HEAD:KV] = vt.astype(BF)
        for d in FARTHEST[:3]:
            near(d, k)

    def distant(d):
        zt = (z + d) % NZ
        arrived(hy.at[zt], rs_recv.at[0, d], to_y)
        fb[zt] = (tf2[zt, y] + hy[zt].astype(F32)).astype(BF)
        send(fb.at[zt], fx.at[zt], rs_send.at[3, d], rs_recv.at[3, d], to_far)

    dq, kt, vt = column(0, dq)
    tf[:, :, :, 0:HEAD] = kt
    tf[:, :, :, HEAD:KV] = vt
    for d in FARTHEST[:3]:
        distant(d)
    for d in FARTHEST[3:]:
        near(d, 1)
        near(d, 2)
        distant(d)
    for h in range(HEADS):
        dq_ref[:, h * HEAD:(h + 1) * HEAD] = dq[h * SLOTS:(h + 1) * SLOTS].astype(BF)
    for d in FARTHEST:
        zt = (z + d) % NZ
        arrived(nl.at[zt], rs_recv.at[1, d], to_left)
        arrived(nr.at[zt], rs_recv.at[2, d], to_right)
        tf[zt] = tf[zt] + nl[zt].astype(F32) + nr[zt].astype(F32)
        arrived(fx.at[zt], rs_recv.at[3, d], to_far)
        tf[zt, y] = tf[zt, y] + fx[zt].astype(F32)
        ub[zt] = tf[zt].astype(BF)
        if d:
            send(ub.at[zt, y], zr.at[z, y], z_send.at[4, d], z_recv.at[4, d], zpeer(d))
        send(ub.at[zt, 1 - y], zr.at[z, y], t_send.at[0, d], t_recv.at[0, d], zpeer_y(d))
    total = tf[z, y]
    arrived(zr.at[z, 1 - y], t_recv.at[0, 0], to_y)
    total = total + zr[z, 1 - y].astype(F32)
    for d in ARRIVE:
        zs = (z + NZ - d) % NZ
        arrived(zr.at[zs, y], z_recv.at[4, d], zpeer(d))
        arrived(zr.at[zs, 1 - y], t_recv.at[0, d], zpeer_y(d))
        total = total + zr[zs, y].astype(F32) + zr[zs, 1 - y].astype(F32)
    gz[z] = total.astype(BF)

    for d in ZORDER:
        send(gz.at[z], gz.at[z], z_send.at[5, d], z_recv.at[5, d], zpeer(d))
    for d in ARRIVE:
        zs = (z + NZ - d) % NZ
        arrived(gz.at[zs], z_recv.at[5, d], zpeer(d))
    slot_grads = gz[...].reshape(NZ * SLOTS, KV)


    def weight_part(r):
        return dot(xz[chunk_of(r)].reshape(NZ * SLOTS, KV), slot_grads, 0, 0).reshape(
            NY, HEAD, KV
        )

    def row_part(xx):
        return dot(slot_grads, wg[xx].reshape(NY * HEAD, KV), 1, 1).reshape(NZ, SLOTS, KV)

    for k in range(2):
        rsb[:, k] = row_part(2 * k + 1 - core).astype(BF)
    for d in FARTHEST:
        zt = (z + d) % NZ
        send(rsb.at[zt], rsr.at[zt], t_send.at[1, d], t_recv.at[1, d], to_sib)
    for r in (2, 1, 3):
        wb[r] = weight_part(r).astype(BF)
        for k in (1, 0):
            send(wb.at[r, half_of(k)], wx.at[r, k], x_send.at[r, k], x_recv.at[r, k], xpeer(r, k))
    for k in range(2):
        rf[:, k] = row_part(2 * k + core)
    for d in FARTHEST:
        zt = (z + d) % NZ
        arrived(rsr.at[zt], t_recv.at[1, d], to_sib)
        ryb[zt] = (rf[zt, 1 - ylo] + rsr[zt, 1 - ylo].astype(F32)).astype(BF)
        send(ryb.at[zt], ryr.at[zt], t_send.at[2, d], t_recv.at[2, d], to_ylo)
    wf[...] = weight_part(0)
    wb[0] = wf[...].astype(BF)
    send(wb.at[0, 1 - y], wx.at[0, 1], x_send.at[0, 1], x_recv.at[0, 1], to_y)
    for d in FARTHEST:
        zt = (z + d) % NZ
        arrived(ryr.at[zt], t_recv.at[2, d], to_ylo)
        tz[zt] = (
            rf[zt, ylo] + rsr[zt, ylo].astype(F32) + ryr[zt].astype(F32)
        ).astype(BF)
        if d:
            send(tz.at[zt], tr.at[z], t_send.at[3, d], t_recv.at[3, d], zpeer(d))
    tr[z] = tz[z]
    for d in ARRIVE:
        zs = (z + NZ - d) % NZ
        arrived(tr.at[zs], t_recv.at[3, d], zpeer(d))
    for zs in range(NZ):
        rows_ref[:, zs * KV:(zs + 1) * KV] = (tr[zs].astype(F32) * live).astype(BF)

    total = wf[y]
    for r, k in XORDER:
        arrived(wx.at[r, k], x_recv.at[r, k], xpeer(NX - r, k))
        total = total + wx[r, k].astype(F32)
    wgr_ref[...] = total.astype(BF)

    for cp in started:
        cp.wait_send()


def finish(
    sel_ref, att_in, dq_in, rows_ref, wgr_ref, att_ref, dq_ref, tg_ref, kwg_ref, vwg_ref
):
    sel_row = jnp.broadcast_to(sel_ref[...], (ROWS, SLOTS))
    place = jnp.where(
        lax.broadcasted_iota(jnp.int32, (ROWS, SLOTS), 0) == sel_row, 1.0, 0.0
    ).astype(BF)
    for k in range(NZ):
        tg_ref[:, k * KV:(k + 1) * KV] = dot(
            place, rows_ref[:, k * KV:(k + 1) * KV], 1, 0
        ).astype(BF)
    att_ref[...] = att_in[...]
    dq_ref[...] = dq_in[...]
    kwg_ref[...] = wgr_ref[:, 0:HEAD]
    vwg_ref[...] = wgr_ref[:, HEAD:KV]


def local(tokens, select_index, valid_count, queries, key_matrix, value_matrix, out_grad):
    vmem = pl.BlockSpec(memory_space=pltpu.VMEM)
    dma = pltpu.SemaphoreType.DMA
    V = pltpu.VMEM
    shape = jax.ShapeDtypeStruct
    block = (NZ, SLOTS, KV)
    pairs = (NZ, NY, SLOTS, KV)
    scratch = [
        V((2, ROWS, NZ * KV), BF),
        V((1, SLOTS), jnp.int32),
        V((1, NX * PER_X), jnp.int32),
        V((SLOTS, HEADS * HEAD), BF),
        V((SLOTS, HEADS * HEAD), BF),
        V((NZ, 2, SLOTS, KV), BF),
        V((NX, NZ, SLOTS, KV), BF),
        V((NX, NY, HEAD, KV), BF),
        V(block, F32),
        V((NZ, SLOTS, HEAD), F32),
        V((NZ, SLOTS, HEAD), BF),
        V((NZ, SLOTS, HEAD), F32),
        V((NZ, SLOTS, HEAD), BF),
        V((NX * PER_X, SLOTS, KV), BF),
        V((QROWS, NX * CHUNK), F32),
        V((QROWS, HEAD), BF),
        V((QROWS, HEAD), BF),
        V(pairs, F32),
        V(pairs, F32),
        V((3,) + pairs, BF),
        V(block, BF),
        V(block, BF),
        V(block, BF),
        V(pairs, BF),
        V(pairs, BF),
        V(pairs, BF),
        V(pairs, BF),
        V(block, BF),
        V((NX, NY, HEAD, KV), BF),
        V((NY, HEAD, KV), F32),
        V((NX, 2, HEAD, KV), BF),
        V((NZ, 2, SLOTS, KV), BF),
        V((NZ, 2, SLOTS, KV), BF),
        V((NZ, 2, SLOTS, KV), F32),
        V(block, BF),
        V(block, BF),
        V(block, BF),
        V(block, BF),
        dma((8,)), dma((NX, 2)), dma((NX, 2)), dma((7, NZ)), dma((7, NZ)), dma((NX, 2)),
        dma((NX, 2)),
        dma((6, NZ)), dma((6, NZ)), dma((4, NZ)), dma((4, NZ)), dma((5, NZ)), dma((5, NZ)),
    ]
    sel = select_index.reshape(1, -1)
    att, dq, rows, wgr = pl.pallas_call(
        kernel,
        out_shape=(
            V((SLOTS, HEADS * HEAD), BF),
            V((SLOTS, HEADS * HEAD), BF),
            V((SLOTS, MODEL // 4), BF),
            V((HEAD, KV), BF),
        ),
        in_specs=[pl.BlockSpec(memory_space=pl.ANY)] * 7,
        out_specs=(vmem,) * 4,
        scratch_shapes=scratch,
        compiler_params=pltpu.CompilerParams(
            collective_id=0, has_side_effects=True, vmem_limit_bytes=62 * 1024 * 1024
        ),
    )(tokens, sel, valid_count.reshape(1, -1), queries, key_matrix, value_matrix, out_grad)
    return pl.pallas_call(
        finish,
        out_shape=(
            shape((SLOTS, HEADS * HEAD), BF),
            shape((SLOTS, HEADS * HEAD), BF),
            shape((ROWS, MODEL // 4), BF),
            shape((HEAD, HEAD), BF),
            shape((HEAD, HEAD), BF),
        ),
        in_specs=[vmem] * 5,
        out_specs=(vmem,) * 5,
        compiler_params=pltpu.CompilerParams(vmem_limit_bytes=6 * 1024 * 1024),
    )(sel, att, dq, rows, wgr)


def solution(mesh):
    in_specs = (
        P("ctx", None), P("ctx"), P(), P("ctx", "tp"), P("ctx", "tp"), P("ctx", "tp"),
        P("ctx", "tp"),
    )
    out_specs = (P("ctx", "tp"),) * 5
    return jax.shard_map(local, mesh=mesh, in_specs=in_specs, out_specs=out_specs, check_vma=False)
```

```python
import math

import jax
import jax.numpy as jnp
from jax import lax
from jax.experimental import pallas as pl
from jax.experimental.pallas import tpu as pltpu
from jax.sharding import PartitionSpec as P

NX, NZ, NY = 4, 8, 2
HEAD = 128
SLOTS = 32
KV = 2 * HEAD
HEADS = 8
ROWS = 256
MODEL = 8192
PER_X = NZ * NY
CHUNK = PER_X * SLOTS
QROWS = HEADS * SLOTS
SCALE = 1.0 / math.sqrt(HEAD)
NEG = -1e30
BF = jnp.bfloat16
F32 = jnp.float32
ZORDER = (4, 3, 5, 2, 6, 1, 7)
ARRIVE = (1, 7, 2, 6, 3, 5, 4)
NEAREST = (0,) + ARRIVE
FARTHEST = ZORDER + (0,)
XORDER = ((2, 1), (2, 0), (1, 1), (3, 1), (1, 0), (3, 0), (0, 1))


def dot(a, b, ca, cb):
    return lax.dot_general(a, b, (((ca,), (cb,)), ((), ())), preferred_element_type=F32)


def kernel(
    tok_hbm, sel_hbm, vc_hbm, q_hbm, wk_hbm, wv_hbm, g_hbm,
    att_ref, dq_ref, rows_ref, wgr_ref,
    tok, sel_ref, vc_ref, q_ref, g_ref, pz, xz, wg, pf, pk, pv, rk, rv, kv, s_ref, qs, gs,
    tf, tf2, tb, hy, fb, fx, nl, nr, ub, zr, gz,
    wb, wf, wf2, why, wfb, wfx, wnl, wnr, wyb, wyr, rsb, rsr, rf, tz, tr,
    in_sem, w_send, w_recv, z_send, z_recv, x_send, x_recv, ag_send, ag_recv, rs_send, rs_recv,
    t_send, t_recv,
):
    c = lax.axis_index("ctx")
    t = lax.axis_index("tp")
    x = c // PER_X
    z = (c // NY) % NZ
    y = c % NY
    core = t % 2
    ylo = t // 2
    right = (x + 1) % NX
    left = (x + NX - 1) % NX
    far = (x + 2) % NX

    def at(xx, zz, yy):
        return {"ctx": (xx * NZ + zz) * NY + yy, "tp": t}

    def zpeer(d):
        return at(x, (z + d) % NZ, y)

    def zpeer_y(d):
        return at(x, (z + d) % NZ, 1 - y)

    def half_of(k):
        return y if k == 0 else 1 - y

    def xpeer(r, k):
        return at((x + r) % NX, z, half_of(k))

    to_right = at(right, z, y)
    to_left = at(left, z, y)
    to_far = at(far, z, y)
    to_y = at(x, z, 1 - y)
    def zpeer_ylo(d):
        return {"ctx": (x * NZ + (z + d) % NZ) * NY + y, "tp": 2 * (1 - ylo) + core}

    to_sib = {"ctx": c, "tp": 2 * ylo + 1 - core}

    started = []

    def copy(src, dst, ssem, rsem, dev):
        return pltpu.make_async_remote_copy(
            src_ref=src, dst_ref=dst, send_sem=ssem, recv_sem=rsem,
            device_id=dev, device_id_type=pl.DeviceIdType.MESH,
        )

    def send(src, dst, ssem, rsem, dev):
        cp = copy(src, dst, ssem, rsem, dev)
        cp.start()
        started.append(cp)

    def arrived(dst, rsem, dev):
        copy(dst, dst, rsem, rsem, dev).wait_recv()

    barrier = pltpu.get_barrier_semaphore()
    partners = [zpeer(d) for d in range(1, NZ)] + [zpeer_y(d) for d in range(1, NZ)]
    partners += [xpeer(r, k) for r in range(1, NX) for k in range(2)] + [to_y, to_sib]
    partners += [zpeer_ylo(d) for d in range(NZ)]
    for dev in partners:
        pl.semaphore_signal(barrier, inc=1, device_id=dev, device_id_type=pl.DeviceIdType.MESH)

    x_cols = NZ * KV
    loads = [pltpu.make_async_copy(sel_hbm, sel_ref, in_sem.at[0])]
    for k in range(2):
        c0 = pl.multiple_of((2 * core + k) * x_cols, x_cols)
        loads.append(
            pltpu.make_async_copy(tok_hbm.at[:, pl.ds(c0, x_cols)], tok.at[k], in_sem.at[1 + k])
        )
    loads.append(pltpu.make_async_copy(wk_hbm, wg.at[x, y, :, pl.ds(0, HEAD)], in_sem.at[3]))
    loads.append(pltpu.make_async_copy(wv_hbm, wg.at[x, y, :, pl.ds(HEAD, HEAD)], in_sem.at[4]))
    loads.append(pltpu.make_async_copy(vc_hbm, vc_ref, in_sem.at[5]))
    loads.append(pltpu.make_async_copy(q_hbm, q_ref, in_sem.at[6]))
    loads.append(pltpu.make_async_copy(g_hbm, g_ref, in_sem.at[7]))
    for cp in loads:
        cp.start()

    loads[0].wait()
    sel_row = jnp.broadcast_to(sel_ref[...], (SLOTS, SLOTS))
    i0 = lax.broadcasted_iota(jnp.int32, (SLOTS, SLOTS), 0)
    i1 = lax.broadcasted_iota(jnp.int32, (SLOTS, SLOTS), 1)
    sel_col = jnp.sum(jnp.where(i0 == i1, sel_row, 0), axis=1, keepdims=True)
    hot = jnp.where(
        lax.broadcasted_iota(jnp.int32, (SLOTS, ROWS), 1) == sel_col, 1.0, 0.0
    ).astype(BF)
    for k in range(2):
        loads[1 + k].wait()
        for zt in range(NZ):
            pz[zt, k] = dot(hot, tok[k, :, zt * KV:(zt + 1) * KV], 1, 0).astype(BF)
    xz[pl.ds(2 * core, 2), z] = pz[z]
    loads[3].wait()
    loads[4].wait()

    pl.semaphore_wait(barrier, len(partners))

    mine = wg.at[x, y]
    for r, k in XORDER:
        send(mine, mine, w_send.at[r, k], w_recv.at[r, k], xpeer(r, k))
    for d in ZORDER:
        send(
            pz.at[(z + d) % NZ], xz.at[pl.ds(2 * core, 2), z],
            z_send.at[0, d], z_recv.at[0, d], zpeer(d),
        )
    send(pz.at[z], xz.at[pl.ds(2 * core, 2), z], z_send.at[1, 0], z_recv.at[1, 0], to_sib)

    for cp in loads[5:]:
        cp.wait()
    vc = vc_ref[...]
    own_count = jnp.sum(
        jnp.where(lax.broadcasted_iota(jnp.int32, vc.shape, 1) == c, vc, 0), axis=1, keepdims=True
    )
    live_col = lax.broadcasted_iota(jnp.int32, (SLOTS, 1), 0) < own_count
    live = jnp.where(live_col, 1.0, 0.0)
    qpos = jnp.where(live_col, sel_col, ROWS).astype(F32)
    qpos_all = jnp.concatenate([qpos] * HEADS, axis=0)
    for h in range(HEADS):
        qs[h * SLOTS:(h + 1) * SLOTS, :] = q_ref[:, h * HEAD:(h + 1) * HEAD]
        gs[h * SLOTS:(h + 1) * SLOTS, :] = (
            g_ref[:, h * HEAD:(h + 1) * HEAD].astype(F32) * live
        ).astype(BF)

    def relay_picked(d):
        zs = (z + NZ - d) % NZ
        block = xz.at[pl.ds(2 * core, 2), zs]
        arrived(block, z_recv.at[0, d], zpeer(d))
        send(block, block, z_send.at[1, d], z_recv.at[1, d], to_sib)

    for d in ARRIVE:
        relay_picked(d)
    for r, k in XORDER:
        arrived(wg.at[(x + NX - r) % NX, half_of(k)], w_recv.at[r, k], xpeer(r, k))
    for d in NEAREST:
        zs = (z + NZ - d) % NZ
        arrived(xz.at[pl.ds(2 * (1 - core), 2), zs], z_recv.at[1, d], to_sib)

    acc = jnp.zeros((NZ * SLOTS, KV), F32)
    for xx in range(NX):
        acc = acc + dot(
            xz[xx].reshape(NZ * SLOTS, KV), wg[xx].reshape(NY * HEAD, KV), 1, 0
        )
    pf[...] = acc.reshape(NZ, SLOTS, KV)
    pk[...] = pf[:, :, 0:HEAD]
    pv[...] = pf[:, :, HEAD:KV].astype(BF)
    for d in ZORDER:
        zt = (z + d) % NZ
        send(pk.at[zt], rk.at[z], z_send.at[2, d], z_recv.at[2, d], zpeer(d))
        send(pv.at[zt], rv.at[z], t_send.at[4, d], t_recv.at[4, d], zpeer(d))
    key_sum = pf[z, :, 0:HEAD]
    value_sum = pf[z, :, HEAD:KV]
    for d in ARRIVE:
        zs = (z + NZ - d) % NZ
        arrived(rk.at[zs], z_recv.at[2, d], zpeer(d))
        key_sum = key_sum + rk[zs]
        arrived(rv.at[zs], t_recv.at[4, d], zpeer(d))
        value_sum = value_sum + rv[zs].astype(F32)
    kv[c, :, 0:HEAD] = key_sum.astype(BF)
    kv[c, :, HEAD:KV] = value_sum.astype(BF)

    def one(xx, zz, yy):
        return kv.at[(xx * NZ + zz) * NY + yy]

    def spread_near(block, d, k):
        send(block, block, ag_send.at[k, d], ag_recv.at[k, d], to_right)
        send(block, block, ag_send.at[k + 1, d], ag_recv.at[k + 1, d], to_left)

    def own_block(d):
        block = one(x, (z + NZ - d) % NZ, y)
        if d:
            arrived(block, z_recv.at[3, d], zpeer(d))
        if d == 4:
            send(block, block, ag_send.at[5, d], ag_recv.at[5, d], xpeer(2, 1))
        send(block, block, ag_send.at[4, d], ag_recv.at[4, d], to_far)
        spread_near(block, d, 0)

    def peer_block(d):
        block = one(x, (z + NZ - d) % NZ, 1 - y)
        arrived(block, z_recv.at[6, d], zpeer_y(d))
        spread_near(block, d, 2)

    def far_block(d):
        block = one(far, (z + NZ - d) % NZ, y)
        arrived(block, ag_recv.at[4, d], to_far)
        if d != 4:
            send(block, block, ag_send.at[5, d], ag_recv.at[5, d], to_y)

    own = one(x, z, y)
    send(own, own, z_send.at[6, 0], z_recv.at[6, 0], to_y)
    for d in ARRIVE:
        send(own, own, z_send.at[3, d], z_recv.at[3, d], zpeer(d))
    own_block(0)
    for d in ARRIVE:
        send(own, own, z_send.at[6, d], z_recv.at[6, d], zpeer_y(d))
    own_block(1)
    own_block(7)
    peer_block(0)
    own_block(2)
    own_block(6)
    far_block(0)
    own_block(3)
    own_block(5)
    peer_block(1)
    peer_block(7)
    own_block(4)
    far_block(1)
    far_block(7)
    peer_block(2)
    peer_block(6)
    far_block(2)
    far_block(6)
    peer_block(3)
    peer_block(5)
    far_block(3)
    far_block(5)
    peer_block(4)
    far_block(4)

    vc8 = jnp.broadcast_to(vc.astype(F32), (8, NX * PER_X)).astype(BF)
    sel8 = jnp.broadcast_to(sel_ref[...].astype(F32), (8, SLOTS)).astype(BF)
    jslot = lax.broadcasted_iota(jnp.int32, (SLOTS, CHUNK), 1) % SLOTS
    spread = jnp.where(jslot == lax.broadcasted_iota(jnp.int32, (SLOTS, CHUNK), 0), 1.0, 0.0)
    sel_keys = dot(sel8, spread.astype(BF), 1, 0)[0:1]
    queries = qs[...]
    grads = gs[...]

    def chunk_of(r):
        return (x + r) % NX

    def keys_of(r):
        return kv[pl.ds(chunk_of(r) * PER_X, PER_X), :, 0:HEAD].reshape(CHUNK, HEAD)

    def values_of(r):
        return kv[pl.ds(chunk_of(r) * PER_X, PER_X), :, HEAD:KV].reshape(CHUNK, HEAD)

    def score(r):
        shard = chunk_of(r) * PER_X + lax.broadcasted_iota(
            jnp.int32, (NX * PER_X, CHUNK), 1
        ) // SLOTS
        expand = jnp.where(
            shard == lax.broadcasted_iota(jnp.int32, (NX * PER_X, CHUNK), 0), 1.0, 0.0
        )
        counts = dot(vc8, expand.astype(BF), 1, 0)[0:1]
        shard_row = chunk_of(r) * PER_X + lax.broadcasted_iota(jnp.int32, (1, CHUNK), 1) // SLOTS
        slot_row = (lax.broadcasted_iota(jnp.int32, (1, CHUNK), 1) % SLOTS).astype(F32)
        place = jnp.where(shard_row < c, -1.0, jnp.where(shard_row > c, 1e6, sel_keys))
        place = jnp.where(slot_row < counts, place, 1e6)
        scores = dot(queries, keys_of(r), 1, 1) * SCALE
        scores = jnp.where(place <= qpos_all, scores, NEG)
        s_ref[:, r * CHUNK:(r + 1) * CHUNK] = scores
        return jnp.max(scores, axis=1, keepdims=True)

    top = score(0)
    for d in NEAREST:
        zs = (z + NZ - d) % NZ
        arrived(one(left, zs, y), ag_recv.at[0, d], to_left)
        arrived(one(right, zs, y), ag_recv.at[1, d], to_right)
        arrived(one(left, zs, 1 - y), ag_recv.at[2, d], to_left)
        arrived(one(right, zs, 1 - y), ag_recv.at[3, d], to_right)
    top = jnp.maximum(top, score(1))
    top = jnp.maximum(top, score(3))
    for d in NEAREST:
        arrived(one(far, (z + NZ - d) % NZ, 1 - y), ag_recv.at[5, d], xpeer(2, 1))
    top = jnp.maximum(top, score(2))
    norm = jnp.zeros((QROWS, 1), F32)
    for r in range(NX):
        terms = jnp.exp(s_ref[:, r * CHUNK:(r + 1) * CHUNK] - top)
        s_ref[:, r * CHUNK:(r + 1) * CHUNK] = terms
        norm = norm + jnp.sum(terms, axis=1, keepdims=True)
    inv = 1.0 / norm
    out = jnp.zeros((QROWS, HEAD), F32)
    for r in range(NX):
        probs = s_ref[:, r * CHUNK:(r + 1) * CHUNK] * inv
        s_ref[:, r * CHUNK:(r + 1) * CHUNK] = probs
        out = out + dot(probs.astype(BF), values_of(r), 1, 0)
    live_all = jnp.concatenate([live] * HEADS, axis=0)
    attended = (out * live_all).astype(BF)
    for h in range(HEADS):
        att_ref[:, h * HEAD:(h + 1) * HEAD] = attended[h * SLOTS:(h + 1) * SLOTS]
    out_dot = jnp.sum(grads.astype(F32) * attended.astype(F32), axis=1, keepdims=True)

    dq = jnp.zeros((QROWS, HEAD), F32)

    def column(r, dq):
        probs = s_ref[:, r * CHUNK:(r + 1) * CHUNK]
        grad_probs = dot(grads, values_of(r), 1, 1)
        ds = (probs * (grad_probs - out_dot) * SCALE).astype(BF)
        dq = dq + dot(ds, keys_of(r), 1, 0)
        kt = dot(ds, queries, 0, 0).reshape(NZ, NY, SLOTS, HEAD)
        vt = dot(probs.astype(BF), grads, 0, 0).reshape(NZ, NY, SLOTS, HEAD)
        return dq, kt, vt

    dq, kt, vt = column(2, dq)
    tf2[:, :, :, 0:HEAD] = kt
    tf2[:, :, :, HEAD:KV] = vt
    tb[0] = tf2[...].astype(BF)
    for d in FARTHEST:
        zt = (z + d) % NZ
        send(tb.at[0, zt, 1 - y], hy.at[zt], rs_send.at[0, d], rs_recv.at[0, d], to_y)
    def near(d, k):
        zt = (z + d) % NZ
        if k == 1:
            send(tb.at[1, zt], nl.at[zt], rs_send.at[1, d], rs_recv.at[1, d], to_right)
        else:
            send(tb.at[2, zt], nr.at[zt], rs_send.at[2, d], rs_recv.at[2, d], to_left)

    for k, r in ((1, 1), (2, 3)):
        dq, kt, vt = column(r, dq)
        tb[k, :, :, :, 0:HEAD] = kt.astype(BF)
        tb[k, :, :, :, HEAD:KV] = vt.astype(BF)
        for d in FARTHEST[:3]:
            near(d, k)

    def distant(d):
        zt = (z + d) % NZ
        arrived(hy.at[zt], rs_recv.at[0, d], to_y)
        fb[zt] = (tf2[zt, y] + hy[zt].astype(F32)).astype(BF)
        send(fb.at[zt], fx.at[zt], rs_send.at[3, d], rs_recv.at[3, d], to_far)

    dq, kt, vt = column(0, dq)
    tf[:, :, :, 0:HEAD] = kt
    tf[:, :, :, HEAD:KV] = vt
    for d in FARTHEST[:3]:
        distant(d)
    for d in FARTHEST[3:]:
        near(d, 1)
        near(d, 2)
        distant(d)
    for h in range(HEADS):
        dq_ref[:, h * HEAD:(h + 1) * HEAD] = dq[h * SLOTS:(h + 1) * SLOTS].astype(BF)
    for d in FARTHEST:
        zt = (z + d) % NZ
        arrived(nl.at[zt], rs_recv.at[1, d], to_left)
        arrived(nr.at[zt], rs_recv.at[2, d], to_right)
        tf[zt] = tf[zt] + nl[zt].astype(F32) + nr[zt].astype(F32)
        arrived(fx.at[zt], rs_recv.at[3, d], to_far)
        tf[zt, y] = tf[zt, y] + fx[zt].astype(F32)
        ub[zt] = tf[zt].astype(BF)
        if d:
            send(ub.at[zt, y], zr.at[z, y], z_send.at[4, d], z_recv.at[4, d], zpeer(d))
        send(ub.at[zt, 1 - y], zr.at[z, y], t_send.at[0, d], t_recv.at[0, d], zpeer_y(d))
    total = tf[z, y]
    arrived(zr.at[z, 1 - y], t_recv.at[0, 0], to_y)
    total = total + zr[z, 1 - y].astype(F32)
    for d in ARRIVE:
        zs = (z + NZ - d) % NZ
        arrived(zr.at[zs, y], z_recv.at[4, d], zpeer(d))
        arrived(zr.at[zs, 1 - y], t_recv.at[0, d], zpeer_y(d))
        total = total + zr[zs, y].astype(F32) + zr[zs, 1 - y].astype(F32)
    gz[z] = total.astype(BF)

    for d in ZORDER:
        send(gz.at[z], gz.at[z], z_send.at[5, d], z_recv.at[5, d], zpeer(d))
    for d in ARRIVE:
        zs = (z + NZ - d) % NZ
        arrived(gz.at[zs], z_recv.at[5, d], zpeer(d))
    slot_grads = gz[...].reshape(NZ * SLOTS, KV)


    def weight_part(r):
        return dot(xz[chunk_of(r)].reshape(NZ * SLOTS, KV), slot_grads, 0, 0).reshape(
            NY, HEAD, KV
        )

    def row_part(xx):
        return dot(slot_grads, wg[xx].reshape(NY * HEAD, KV), 1, 1).reshape(NZ, SLOTS, KV)

    for k in range(2):
        rsb[:, k] = row_part(2 * k + 1 - core).astype(BF)
    for d in FARTHEST:
        zt = (z + d) % NZ
        send(rsb.at[zt], rsr.at[zt], t_send.at[1, d], t_recv.at[1, d], to_sib)
    wf2[...] = weight_part(2)
    wb[0] = wf2[...].astype(BF)
    send(wb.at[0, 1 - y], why, x_send.at[0, 0], x_recv.at[0, 0], to_y)
    wb[1] = weight_part(1).astype(BF)
    send(wb.at[1], wnl, x_send.at[1, 0], x_recv.at[1, 0], to_right)
    wb[2] = weight_part(3).astype(BF)
    send(wb.at[2], wnr, x_send.at[2, 0], x_recv.at[2, 0], to_left)
    for k in range(2):
        rf[:, k] = row_part(2 * k + core)
    for d in FARTHEST:
        zt = (z + d) % NZ
        arrived(rsr.at[zt], t_recv.at[1, d], to_sib)
        tz[zt] = (rf[zt] + rsr[zt].astype(F32)).astype(BF)
        send(tz.at[zt, 1 - ylo], tr.at[z, 1], t_send.at[2, d], t_recv.at[2, d], zpeer_ylo(d))
        if d:
            send(tz.at[zt, ylo], tr.at[z, 0], t_send.at[3, d], t_recv.at[3, d], zpeer(d))
    tr[z, 0] = tz[z, ylo]
    wf[...] = weight_part(0)
    arrived(why, x_recv.at[0, 0], to_y)
    wfb[...] = (wf2[y] + why[...].astype(F32)).astype(BF)
    send(wfb, wfx, x_send.at[3, 0], x_recv.at[3, 0], to_far)
    arrived(wnl, x_recv.at[1, 0], to_left)
    arrived(wnr, x_recv.at[2, 0], to_right)
    wf[...] = wf[...] + wnl[...].astype(F32) + wnr[...].astype(F32)
    wyb[...] = wf[1 - y].astype(BF)
    send(wyb, wyr, x_send.at[0, 1], x_recv.at[0, 1], to_y)

    for d in NEAREST:
        zs = (z + NZ - d) % NZ
        arrived(tr.at[zs, 1], t_recv.at[2, d], zpeer_ylo(d))
        if d:
            arrived(tr.at[zs, 0], t_recv.at[3, d], zpeer(d))
    for zs in range(NZ):
        both = tr[zs, 0].astype(F32) + tr[zs, 1].astype(F32)
        rows_ref[:, zs * KV:(zs + 1) * KV] = (both * live).astype(BF)

    arrived(wfx, x_recv.at[3, 0], to_far)
    arrived(wyr, x_recv.at[0, 1], to_y)
    wgr_ref[...] = (wf[y] + wfx[...].astype(F32) + wyr[...].astype(F32)).astype(BF)

    for cp in started:
        cp.wait_send()


def finish(
    sel_ref, att_in, dq_in, rows_ref, wgr_ref, att_ref, dq_ref, tg_ref, kwg_ref, vwg_ref
):
    sel_row = jnp.broadcast_to(sel_ref[...], (ROWS, SLOTS))
    place = jnp.where(
        lax.broadcasted_iota(jnp.int32, (ROWS, SLOTS), 0) == sel_row, 1.0, 0.0
    ).astype(BF)
    for k in range(NZ):
        tg_ref[:, k * KV:(k + 1) * KV] = dot(
            place, rows_ref[:, k * KV:(k + 1) * KV], 1, 0
        ).astype(BF)
    att_ref[...] = att_in[...]
    dq_ref[...] = dq_in[...]
    kwg_ref[...] = wgr_ref[:, 0:HEAD]
    vwg_ref[...] = wgr_ref[:, HEAD:KV]


def local(tokens, select_index, valid_count, queries, key_matrix, value_matrix, out_grad):
    vmem = pl.BlockSpec(memory_space=pltpu.VMEM)
    dma = pltpu.SemaphoreType.DMA
    V = pltpu.VMEM
    shape = jax.ShapeDtypeStruct
    block = (NZ, SLOTS, KV)
    pairs = (NZ, NY, SLOTS, KV)
    scratch = [
        V((2, ROWS, NZ * KV), BF),
        V((1, SLOTS), jnp.int32),
        V((1, NX * PER_X), jnp.int32),
        V((SLOTS, HEADS * HEAD), BF),
        V((SLOTS, HEADS * HEAD), BF),
        V((NZ, 2, SLOTS, KV), BF),
        V((NX, NZ, SLOTS, KV), BF),
        V((NX, NY, HEAD, KV), BF),
        V(block, F32),
        V((NZ, SLOTS, HEAD), F32),
        V((NZ, SLOTS, HEAD), BF),
        V((NZ, SLOTS, HEAD), F32),
        V((NZ, SLOTS, HEAD), BF),
        V((NX * PER_X, SLOTS, KV), BF),
        V((QROWS, NX * CHUNK), F32),
        V((QROWS, HEAD), BF),
        V((QROWS, HEAD), BF),
        V(pairs, F32),
        V(pairs, F32),
        V((3,) + pairs, BF),
        V(block, BF),
        V(block, BF),
        V(block, BF),
        V(pairs, BF),
        V(pairs, BF),
        V(pairs, BF),
        V(pairs, BF),
        V(block, BF),
        V((3, NY, HEAD, KV), BF),
        V((NY, HEAD, KV), F32),
        V((NY, HEAD, KV), F32),
        V((HEAD, KV), BF),
        V((HEAD, KV), BF),
        V((HEAD, KV), BF),
        V((NY, HEAD, KV), BF),
        V((NY, HEAD, KV), BF),
        V((HEAD, KV), BF),
        V((HEAD, KV), BF),
        V((NZ, 2, SLOTS, KV), BF),
        V((NZ, 2, SLOTS, KV), BF),
        V((NZ, 2, SLOTS, KV), F32),
        V((NZ, 2, SLOTS, KV), BF),
        V((NZ, 2, SLOTS, KV), BF),
        dma((8,)), dma((NX, 2)), dma((NX, 2)), dma((7, NZ)), dma((7, NZ)), dma((NX, 2)),
        dma((NX, 2)),
        dma((6, NZ)), dma((6, NZ)), dma((4, NZ)), dma((4, NZ)), dma((5, NZ)), dma((5, NZ)),
    ]
    sel = select_index.reshape(1, -1)
    att, dq, rows, wgr = pl.pallas_call(
        kernel,
        out_shape=(
            V((SLOTS, HEADS * HEAD), BF),
            V((SLOTS, HEADS * HEAD), BF),
            V((SLOTS, MODEL // 4), BF),
            V((HEAD, KV), BF),
        ),
        in_specs=[pl.BlockSpec(memory_space=pl.ANY)] * 7,
        out_specs=(vmem,) * 4,
        scratch_shapes=scratch,
        compiler_params=pltpu.CompilerParams(
            collective_id=0, has_side_effects=True, vmem_limit_bytes=62 * 1024 * 1024
        ),
    )(tokens, sel, valid_count.reshape(1, -1), queries, key_matrix, value_matrix, out_grad)
    return pl.pallas_call(
        finish,
        out_shape=(
            shape((SLOTS, HEADS * HEAD), BF),
            shape((SLOTS, HEADS * HEAD), BF),
            shape((ROWS, MODEL // 4), BF),
            shape((HEAD, HEAD), BF),
            shape((HEAD, HEAD), BF),
        ),
        in_specs=[vmem] * 5,
        out_specs=(vmem,) * 5,
        compiler_params=pltpu.CompilerParams(vmem_limit_bytes=6 * 1024 * 1024),
    )(sel, att, dq, rows, wgr)


def solution(mesh):
    in_specs = (
        P("ctx", None), P("ctx"), P(), P("ctx", "tp"), P("ctx", "tp"), P("ctx", "tp"),
        P("ctx", "tp"),
    )
    out_specs = (P("ctx", "tp"),) * 5
    return jax.shard_map(local, mesh=mesh, in_specs=in_specs, out_specs=out_specs, check_vma=False)
```

```python
import math

import jax
import jax.numpy as jnp
from jax import lax
from jax.experimental import pallas as pl
from jax.experimental.pallas import tpu as pltpu
from jax.sharding import PartitionSpec as P

NX, NZ, NY = 4, 8, 2
HEAD = 128
SLOTS = 32
KV = 2 * HEAD
HEADS = 8
ROWS = 256
MODEL = 8192
PER_X = NZ * NY
CHUNK = PER_X * SLOTS
QROWS = HEADS * SLOTS
SCALE = 1.0 / math.sqrt(HEAD)
NEG = -1e30
BF = jnp.bfloat16
F32 = jnp.float32
ZORDER = (4, 3, 5, 2, 6, 1, 7)
ARRIVE = (1, 7, 2, 6, 3, 5, 4)
NEAREST = (0,) + ARRIVE
FARTHEST = ZORDER + (0,)
XORDER = ((2, 1), (2, 0), (1, 1), (3, 1), (1, 0), (3, 0), (0, 1))


def dot(a, b, ca, cb):
    return lax.dot_general(a, b, (((ca,), (cb,)), ((), ())), preferred_element_type=F32)


def kernel(
    tok_hbm, sel_hbm, vc_hbm, q_hbm, wk_hbm, wv_hbm, g_hbm,
    att_ref, dq_ref, rows_ref, wgr_ref,
    tok, sel_ref, vc_ref, q_ref, g_ref, pz, xz, wg, pf, pk, pv, rk, rv, kv, s_ref, qs, gs,
    tf, tf2, tb, hy, fb, fx, nl, nr, ub, zr, gz,
    wb, wf, wf2, why, wfb, wfx, wnl, wnr, wyb, wyr, rsb, rsr, rf, tz, tr,
    in_sem, w_send, w_recv, z_send, z_recv, x_send, x_recv, ag_send, ag_recv, rs_send, rs_recv,
    t_send, t_recv,
):
    c = lax.axis_index("ctx")
    t = lax.axis_index("tp")
    x = c // PER_X
    z = (c // NY) % NZ
    y = c % NY
    core = t % 2
    ylo = t // 2
    right = (x + 1) % NX
    left = (x + NX - 1) % NX
    far = (x + 2) % NX

    def at(xx, zz, yy):
        return {"ctx": (xx * NZ + zz) * NY + yy, "tp": t}

    def zpeer(d):
        return at(x, (z + d) % NZ, y)

    def zpeer_y(d):
        return at(x, (z + d) % NZ, 1 - y)

    def half_of(k):
        return y if k == 0 else 1 - y

    def xpeer(r, k):
        return at((x + r) % NX, z, half_of(k))

    to_right = at(right, z, y)
    to_left = at(left, z, y)
    to_far = at(far, z, y)
    to_y = at(x, z, 1 - y)
    def zpeer_ylo(d):
        return {"ctx": (x * NZ + (z + d) % NZ) * NY + y, "tp": 2 * (1 - ylo) + core}

    to_sib = {"ctx": c, "tp": 2 * ylo + 1 - core}

    started = []

    def copy(src, dst, ssem, rsem, dev):
        return pltpu.make_async_remote_copy(
            src_ref=src, dst_ref=dst, send_sem=ssem, recv_sem=rsem,
            device_id=dev, device_id_type=pl.DeviceIdType.MESH,
        )

    def send(src, dst, ssem, rsem, dev):
        cp = copy(src, dst, ssem, rsem, dev)
        cp.start()
        started.append(cp)

    def drain(count):
        for cp in started[:count]:
            cp.wait_send()
        del started[:count]

    def arrived(dst, rsem, dev):
        copy(dst, dst, rsem, rsem, dev).wait_recv()

    barrier = pltpu.get_barrier_semaphore()
    partners = [zpeer(d) for d in range(1, NZ)] + [zpeer_y(d) for d in range(1, NZ)]
    partners += [xpeer(r, k) for r in range(1, NX) for k in range(2)] + [to_y, to_sib]
    partners += [zpeer_ylo(d) for d in range(NZ)]
    for dev in partners:
        pl.semaphore_signal(barrier, inc=1, device_id=dev, device_id_type=pl.DeviceIdType.MESH)

    x_cols = NZ * KV
    loads = [pltpu.make_async_copy(sel_hbm, sel_ref, in_sem.at[0])]
    for k in range(2):
        c0 = pl.multiple_of((2 * core + k) * x_cols, x_cols)
        loads.append(
            pltpu.make_async_copy(tok_hbm.at[:, pl.ds(c0, x_cols)], tok.at[k], in_sem.at[1 + k])
        )
    loads.append(pltpu.make_async_copy(wk_hbm, wg.at[x, y, :, pl.ds(0, HEAD)], in_sem.at[3]))
    loads.append(pltpu.make_async_copy(wv_hbm, wg.at[x, y, :, pl.ds(HEAD, HEAD)], in_sem.at[4]))
    loads.append(pltpu.make_async_copy(vc_hbm, vc_ref, in_sem.at[5]))
    loads.append(pltpu.make_async_copy(q_hbm, q_ref, in_sem.at[6]))
    loads.append(pltpu.make_async_copy(g_hbm, g_ref, in_sem.at[7]))
    for cp in loads:
        cp.start()

    loads[0].wait()
    sel_row = jnp.broadcast_to(sel_ref[...], (SLOTS, SLOTS))
    i0 = lax.broadcasted_iota(jnp.int32, (SLOTS, SLOTS), 0)
    i1 = lax.broadcasted_iota(jnp.int32, (SLOTS, SLOTS), 1)
    sel_col = jnp.sum(jnp.where(i0 == i1, sel_row, 0), axis=1, keepdims=True)
    hot = jnp.where(
        lax.broadcasted_iota(jnp.int32, (SLOTS, ROWS), 1) == sel_col, 1.0, 0.0
    ).astype(BF)
    for k in range(2):
        loads[1 + k].wait()
        for zt in range(NZ):
            pz[zt, k] = dot(hot, tok[k, :, zt * KV:(zt + 1) * KV], 1, 0).astype(BF)
    xz[pl.ds(2 * core, 2), z] = pz[z]
    loads[3].wait()
    loads[4].wait()

    pl.semaphore_wait(barrier, len(partners))

    mine = wg.at[x, y]
    for r, k in XORDER:
        send(mine, mine, w_send.at[r, k], w_recv.at[r, k], xpeer(r, k))
    for d in ZORDER:
        send(
            pz.at[(z + d) % NZ], xz.at[pl.ds(2 * core, 2), z],
            z_send.at[0, d], z_recv.at[0, d], zpeer(d),
        )
    send(pz.at[z], xz.at[pl.ds(2 * core, 2), z], z_send.at[1, 0], z_recv.at[1, 0], to_sib)

    for cp in loads[5:]:
        cp.wait()
    vc = vc_ref[...]
    own_count = jnp.sum(
        jnp.where(lax.broadcasted_iota(jnp.int32, vc.shape, 1) == c, vc, 0), axis=1, keepdims=True
    )
    live_col = lax.broadcasted_iota(jnp.int32, (SLOTS, 1), 0) < own_count
    live = jnp.where(live_col, 1.0, 0.0)
    qpos = jnp.where(live_col, sel_col, ROWS).astype(F32)
    qpos_all = jnp.concatenate([qpos] * HEADS, axis=0)
    for h in range(HEADS):
        qs[h * SLOTS:(h + 1) * SLOTS, :] = q_ref[:, h * HEAD:(h + 1) * HEAD]
        gs[h * SLOTS:(h + 1) * SLOTS, :] = (
            g_ref[:, h * HEAD:(h + 1) * HEAD].astype(F32) * live
        ).astype(BF)

    def relay_picked(d):
        zs = (z + NZ - d) % NZ
        block = xz.at[pl.ds(2 * core, 2), zs]
        arrived(block, z_recv.at[0, d], zpeer(d))
        send(block, block, z_send.at[1, d], z_recv.at[1, d], to_sib)

    for d in ARRIVE:
        relay_picked(d)
    for r, k in XORDER:
        arrived(wg.at[(x + NX - r) % NX, half_of(k)], w_recv.at[r, k], xpeer(r, k))
    for d in NEAREST:
        zs = (z + NZ - d) % NZ
        arrived(xz.at[pl.ds(2 * (1 - core), 2), zs], z_recv.at[1, d], to_sib)

    acc = jnp.zeros((NZ * SLOTS, KV), F32)
    for xx in range(NX):
        acc = acc + dot(
            xz[xx].reshape(NZ * SLOTS, KV), wg[xx].reshape(NY * HEAD, KV), 1, 0
        )
    earlier = len(started)
    pf[...] = acc.reshape(NZ, SLOTS, KV)
    pk[...] = pf[:, :, 0:HEAD]
    pv[...] = pf[:, :, HEAD:KV].astype(BF)
    for d in ZORDER:
        zt = (z + d) % NZ
        send(pk.at[zt], rk.at[z], z_send.at[2, d], z_recv.at[2, d], zpeer(d))
        send(pv.at[zt], rv.at[z], t_send.at[4, d], t_recv.at[4, d], zpeer(d))
    drain(earlier)
    key_sum = pf[z, :, 0:HEAD]
    value_sum = pf[z, :, HEAD:KV]
    for d in ARRIVE:
        zs = (z + NZ - d) % NZ
        arrived(rk.at[zs], z_recv.at[2, d], zpeer(d))
        key_sum = key_sum + rk[zs]
        arrived(rv.at[zs], t_recv.at[4, d], zpeer(d))
        value_sum = value_sum + rv[zs].astype(F32)
    kv[c, :, 0:HEAD] = key_sum.astype(BF)
    kv[c, :, HEAD:KV] = value_sum.astype(BF)

    def one(xx, zz, yy):
        return kv.at[(xx * NZ + zz) * NY + yy]

    def spread_near(block, d, k):
        send(block, block, ag_send.at[k, d], ag_recv.at[k, d], to_right)
        send(block, block, ag_send.at[k + 1, d], ag_recv.at[k + 1, d], to_left)

    def own_block(d):
        block = one(x, (z + NZ - d) % NZ, y)
        if d:
            arrived(block, z_recv.at[3, d], zpeer(d))
        if d == 4:
            send(block, block, ag_send.at[5, d], ag_recv.at[5, d], xpeer(2, 1))
        send(block, block, ag_send.at[4, d], ag_recv.at[4, d], to_far)
        spread_near(block, d, 0)

    def peer_block(d):
        block = one(x, (z + NZ - d) % NZ, 1 - y)
        arrived(block, z_recv.at[6, d], zpeer_y(d))
        spread_near(block, d, 2)

    def far_block(d):
        block = one(far, (z + NZ - d) % NZ, y)
        arrived(block, ag_recv.at[4, d], to_far)
        if d != 4:
            send(block, block, ag_send.at[5, d], ag_recv.at[5, d], to_y)

    own = one(x, z, y)
    send(own, own, z_send.at[6, 0], z_recv.at[6, 0], to_y)
    for d in ARRIVE:
        send(own, own, z_send.at[3, d], z_recv.at[3, d], zpeer(d))
    own_block(0)
    for d in ARRIVE:
        send(own, own, z_send.at[6, d], z_recv.at[6, d], zpeer_y(d))
    own_block(1)
    own_block(7)
    peer_block(0)
    own_block(2)
    own_block(6)
    far_block(0)
    own_block(3)
    own_block(5)
    peer_block(1)
    peer_block(7)
    own_block(4)
    far_block(1)
    far_block(7)
    peer_block(2)
    peer_block(6)
    far_block(2)
    far_block(6)
    peer_block(3)
    peer_block(5)
    far_block(3)
    far_block(5)
    peer_block(4)
    far_block(4)

    vc8 = jnp.broadcast_to(vc.astype(F32), (8, NX * PER_X)).astype(BF)
    sel8 = jnp.broadcast_to(sel_ref[...].astype(F32), (8, SLOTS)).astype(BF)
    jslot = lax.broadcasted_iota(jnp.int32, (SLOTS, CHUNK), 1) % SLOTS
    spread = jnp.where(jslot == lax.broadcasted_iota(jnp.int32, (SLOTS, CHUNK), 0), 1.0, 0.0)
    sel_keys = dot(sel8, spread.astype(BF), 1, 0)[0:1]
    queries = qs[...]
    grads = gs[...]

    def chunk_of(r):
        return (x + r) % NX

    def keys_of(r):
        return kv[pl.ds(chunk_of(r) * PER_X, PER_X), :, 0:HEAD].reshape(CHUNK, HEAD)

    def values_of(r):
        return kv[pl.ds(chunk_of(r) * PER_X, PER_X), :, HEAD:KV].reshape(CHUNK, HEAD)

    def score(r):
        shard = chunk_of(r) * PER_X + lax.broadcasted_iota(
            jnp.int32, (NX * PER_X, CHUNK), 1
        ) // SLOTS
        expand = jnp.where(
            shard == lax.broadcasted_iota(jnp.int32, (NX * PER_X, CHUNK), 0), 1.0, 0.0
        )
        counts = dot(vc8, expand.astype(BF), 1, 0)[0:1]
        shard_row = chunk_of(r) * PER_X + lax.broadcasted_iota(jnp.int32, (1, CHUNK), 1) // SLOTS
        slot_row = (lax.broadcasted_iota(jnp.int32, (1, CHUNK), 1) % SLOTS).astype(F32)
        place = jnp.where(shard_row < c, -1.0, jnp.where(shard_row > c, 1e6, sel_keys))
        place = jnp.where(slot_row < counts, place, 1e6)
        scores = dot(queries, keys_of(r), 1, 1) * SCALE
        scores = jnp.where(place <= qpos_all, scores, NEG)
        s_ref[:, r * CHUNK:(r + 1) * CHUNK] = scores
        return jnp.max(scores, axis=1, keepdims=True)

    top = score(0)
    for d in NEAREST:
        zs = (z + NZ - d) % NZ
        arrived(one(left, zs, y), ag_recv.at[0, d], to_left)
        arrived(one(right, zs, y), ag_recv.at[1, d], to_right)
        arrived(one(left, zs, 1 - y), ag_recv.at[2, d], to_left)
        arrived(one(right, zs, 1 - y), ag_recv.at[3, d], to_right)
    top = jnp.maximum(top, score(1))
    top = jnp.maximum(top, score(3))
    for d in NEAREST:
        arrived(one(far, (z + NZ - d) % NZ, 1 - y), ag_recv.at[5, d], xpeer(2, 1))
    top = jnp.maximum(top, score(2))
    norm = jnp.zeros((QROWS, 1), F32)
    for r in range(NX):
        terms = jnp.exp(s_ref[:, r * CHUNK:(r + 1) * CHUNK] - top)
        s_ref[:, r * CHUNK:(r + 1) * CHUNK] = terms
        norm = norm + jnp.sum(terms, axis=1, keepdims=True)
    inv = 1.0 / norm
    out = jnp.zeros((QROWS, HEAD), F32)
    for r in range(NX):
        probs = s_ref[:, r * CHUNK:(r + 1) * CHUNK] * inv
        s_ref[:, r * CHUNK:(r + 1) * CHUNK] = probs
        out = out + dot(probs.astype(BF), values_of(r), 1, 0)
    live_all = jnp.concatenate([live] * HEADS, axis=0)
    attended = (out * live_all).astype(BF)
    for h in range(HEADS):
        att_ref[:, h * HEAD:(h + 1) * HEAD] = attended[h * SLOTS:(h + 1) * SLOTS]
    out_dot = jnp.sum(grads.astype(F32) * attended.astype(F32), axis=1, keepdims=True)

    earlier = len(started)
    dq = jnp.zeros((QROWS, HEAD), F32)

    def column(r, dq):
        probs = s_ref[:, r * CHUNK:(r + 1) * CHUNK]
        grad_probs = dot(grads, values_of(r), 1, 1)
        ds = (probs * (grad_probs - out_dot) * SCALE).astype(BF)
        dq = dq + dot(ds, keys_of(r), 1, 0)
        kt = dot(ds, queries, 0, 0).reshape(NZ, NY, SLOTS, HEAD)
        vt = dot(probs.astype(BF), grads, 0, 0).reshape(NZ, NY, SLOTS, HEAD)
        return dq, kt, vt

    dq, kt, vt = column(2, dq)
    tf2[:, :, :, 0:HEAD] = kt
    tf2[:, :, :, HEAD:KV] = vt
    tb[0] = tf2[...].astype(BF)
    for d in FARTHEST:
        zt = (z + d) % NZ
        send(tb.at[0, zt, 1 - y], hy.at[zt], rs_send.at[0, d], rs_recv.at[0, d], to_y)
    def near(d, k):
        zt = (z + d) % NZ
        if k == 1:
            send(tb.at[1, zt], nl.at[zt], rs_send.at[1, d], rs_recv.at[1, d], to_right)
        else:
            send(tb.at[2, zt], nr.at[zt], rs_send.at[2, d], rs_recv.at[2, d], to_left)

    for k, r in ((1, 1), (2, 3)):
        dq, kt, vt = column(r, dq)
        tb[k, :, :, :, 0:HEAD] = kt.astype(BF)
        tb[k, :, :, :, HEAD:KV] = vt.astype(BF)
        for d in FARTHEST[:3]:
            near(d, k)

    def distant(d):
        zt = (z + d) % NZ
        arrived(hy.at[zt], rs_recv.at[0, d], to_y)
        fb[zt] = (tf2[zt, y] + hy[zt].astype(F32)).astype(BF)
        send(fb.at[zt], fx.at[zt], rs_send.at[3, d], rs_recv.at[3, d], to_far)

    dq, kt, vt = column(0, dq)
    tf[:, :, :, 0:HEAD] = kt
    tf[:, :, :, HEAD:KV] = vt
    for d in FARTHEST[:3]:
        distant(d)
    for d in FARTHEST[3:]:
        near(d, 1)
        near(d, 2)
        distant(d)
    for h in range(HEADS):
        dq_ref[:, h * HEAD:(h + 1) * HEAD] = dq[h * SLOTS:(h + 1) * SLOTS].astype(BF)
    for d in FARTHEST:
        zt = (z + d) % NZ
        arrived(nl.at[zt], rs_recv.at[1, d], to_left)
        arrived(nr.at[zt], rs_recv.at[2, d], to_right)
        tf[zt] = tf[zt] + nl[zt].astype(F32) + nr[zt].astype(F32)
        arrived(fx.at[zt], rs_recv.at[3, d], to_far)
        tf[zt, y] = tf[zt, y] + fx[zt].astype(F32)
        ub[zt] = tf[zt].astype(BF)
        if d:
            send(ub.at[zt, y], zr.at[z, y], z_send.at[4, d], z_recv.at[4, d], zpeer(d))
        send(ub.at[zt, 1 - y], zr.at[z, y], t_send.at[0, d], t_recv.at[0, d], zpeer_y(d))
    drain(earlier)
    total = tf[z, y]
    arrived(zr.at[z, 1 - y], t_recv.at[0, 0], to_y)
    total = total + zr[z, 1 - y].astype(F32)
    for d in ARRIVE:
        zs = (z + NZ - d) % NZ
        arrived(zr.at[zs, y], z_recv.at[4, d], zpeer(d))
        arrived(zr.at[zs, 1 - y], t_recv.at[0, d], zpeer_y(d))
        total = total + zr[zs, y].astype(F32) + zr[zs, 1 - y].astype(F32)
    gz[z] = total.astype(BF)

    earlier = len(started)
    for d in ZORDER:
        send(gz.at[z], gz.at[z], z_send.at[5, d], z_recv.at[5, d], zpeer(d))
    drain(earlier)
    earlier = len(started)
    for d in ARRIVE:
        zs = (z + NZ - d) % NZ
        arrived(gz.at[zs], z_recv.at[5, d], zpeer(d))
    slot_grads = gz[...].reshape(NZ * SLOTS, KV)


    def weight_part(r):
        return dot(xz[chunk_of(r)].reshape(NZ * SLOTS, KV), slot_grads, 0, 0).reshape(
            NY, HEAD, KV
        )

    def row_part(xx):
        return dot(slot_grads, wg[xx].reshape(NY * HEAD, KV), 1, 1).reshape(NZ, SLOTS, KV)

    for k in range(2):
        rsb[:, k] = row_part(2 * k + 1 - core).astype(BF)
    for d in FARTHEST:
        zt = (z + d) % NZ
        send(rsb.at[zt], rsr.at[zt], t_send.at[1, d], t_recv.at[1, d], to_sib)
    wf2[...] = weight_part(2)
    wb[0] = wf2[...].astype(BF)
    send(wb.at[0, 1 - y], why, x_send.at[0, 0], x_recv.at[0, 0], to_y)
    wb[1] = weight_part(1).astype(BF)
    send(wb.at[1], wnl, x_send.at[1, 0], x_recv.at[1, 0], to_right)
    wb[2] = weight_part(3).astype(BF)
    send(wb.at[2], wnr, x_send.at[2, 0], x_recv.at[2, 0], to_left)
    for k in range(2):
        rf[:, k] = row_part(2 * k + core)
    for d in FARTHEST:
        zt = (z + d) % NZ
        arrived(rsr.at[zt], t_recv.at[1, d], to_sib)
        tz[zt] = (rf[zt] + rsr[zt].astype(F32)).astype(BF)
        send(tz.at[zt, 1 - ylo], tr.at[z, 1], t_send.at[2, d], t_recv.at[2, d], zpeer_ylo(d))
        if d:
            send(tz.at[zt, ylo], tr.at[z, 0], t_send.at[3, d], t_recv.at[3, d], zpeer(d))
    tr[z, 0] = tz[z, ylo]
    wf[...] = weight_part(0)
    arrived(why, x_recv.at[0, 0], to_y)
    wfb[...] = (wf2[y] + why[...].astype(F32)).astype(BF)
    send(wfb, wfx, x_send.at[3, 0], x_recv.at[3, 0], to_far)
    arrived(wnl, x_recv.at[1, 0], to_left)
    arrived(wnr, x_recv.at[2, 0], to_right)
    wf[...] = wf[...] + wnl[...].astype(F32) + wnr[...].astype(F32)
    wyb[...] = wf[1 - y].astype(BF)
    send(wyb, wyr, x_send.at[0, 1], x_recv.at[0, 1], to_y)

    drain(earlier)

    for d in NEAREST:
        zs = (z + NZ - d) % NZ
        arrived(tr.at[zs, 1], t_recv.at[2, d], zpeer_ylo(d))
        if d:
            arrived(tr.at[zs, 0], t_recv.at[3, d], zpeer(d))
    for zs in range(NZ):
        both = tr[zs, 0].astype(F32) + tr[zs, 1].astype(F32)
        rows_ref[:, zs * KV:(zs + 1) * KV] = (both * live).astype(BF)

    arrived(wfx, x_recv.at[3, 0], to_far)
    arrived(wyr, x_recv.at[0, 1], to_y)
    wgr_ref[...] = (wf[y] + wfx[...].astype(F32) + wyr[...].astype(F32)).astype(BF)

    drain(len(started))


def finish(
    sel_ref, att_in, dq_in, rows_ref, wgr_ref, att_ref, dq_ref, tg_ref, kwg_ref, vwg_ref
):
    sel_row = jnp.broadcast_to(sel_ref[...], (ROWS, SLOTS))
    place = jnp.where(
        lax.broadcasted_iota(jnp.int32, (ROWS, SLOTS), 0) == sel_row, 1.0, 0.0
    ).astype(BF)
    for k in range(NZ):
        tg_ref[:, k * KV:(k + 1) * KV] = dot(
            place, rows_ref[:, k * KV:(k + 1) * KV], 1, 0
        ).astype(BF)
    att_ref[...] = att_in[...]
    dq_ref[...] = dq_in[...]
    kwg_ref[...] = wgr_ref[:, 0:HEAD]
    vwg_ref[...] = wgr_ref[:, HEAD:KV]


def local(tokens, select_index, valid_count, queries, key_matrix, value_matrix, out_grad):
    vmem = pl.BlockSpec(memory_space=pltpu.VMEM)
    dma = pltpu.SemaphoreType.DMA
    V = pltpu.VMEM
    shape = jax.ShapeDtypeStruct
    block = (NZ, SLOTS, KV)
    pairs = (NZ, NY, SLOTS, KV)
    scratch = [
        V((2, ROWS, NZ * KV), BF),
        V((1, SLOTS), jnp.int32),
        V((1, NX * PER_X), jnp.int32),
        V((SLOTS, HEADS * HEAD), BF),
        V((SLOTS, HEADS * HEAD), BF),
        V((NZ, 2, SLOTS, KV), BF),
        V((NX, NZ, SLOTS, KV), BF),
        V((NX, NY, HEAD, KV), BF),
        V(block, F32),
        V((NZ, SLOTS, HEAD), F32),
        V((NZ, SLOTS, HEAD), BF),
        V((NZ, SLOTS, HEAD), F32),
        V((NZ, SLOTS, HEAD), BF),
        V((NX * PER_X, SLOTS, KV), BF),
        V((QROWS, NX * CHUNK), F32),
        V((QROWS, HEAD), BF),
        V((QROWS, HEAD), BF),
        V(pairs, F32),
        V(pairs, F32),
        V((3,) + pairs, BF),
        V(block, BF),
        V(block, BF),
        V(block, BF),
        V(pairs, BF),
        V(pairs, BF),
        V(pairs, BF),
        V(pairs, BF),
        V(block, BF),
        V((3, NY, HEAD, KV), BF),
        V((NY, HEAD, KV), F32),
        V((NY, HEAD, KV), F32),
        V((HEAD, KV), BF),
        V((HEAD, KV), BF),
        V((HEAD, KV), BF),
        V((NY, HEAD, KV), BF),
        V((NY, HEAD, KV), BF),
        V((HEAD, KV), BF),
        V((HEAD, KV), BF),
        V((NZ, 2, SLOTS, KV), BF),
        V((NZ, 2, SLOTS, KV), BF),
        V((NZ, 2, SLOTS, KV), F32),
        V((NZ, 2, SLOTS, KV), BF),
        V((NZ, 2, SLOTS, KV), BF),
        dma((8,)), dma((NX, 2)), dma((NX, 2)), dma((7, NZ)), dma((7, NZ)), dma((NX, 2)),
        dma((NX, 2)),
        dma((6, NZ)), dma((6, NZ)), dma((4, NZ)), dma((4, NZ)), dma((5, NZ)), dma((5, NZ)),
    ]
    sel = select_index.reshape(1, -1)
    att, dq, rows, wgr = pl.pallas_call(
        kernel,
        out_shape=(
            V((SLOTS, HEADS * HEAD), BF),
            V((SLOTS, HEADS * HEAD), BF),
            V((SLOTS, MODEL // 4), BF),
            V((HEAD, KV), BF),
        ),
        in_specs=[pl.BlockSpec(memory_space=pl.ANY)] * 7,
        out_specs=(vmem,) * 4,
        scratch_shapes=scratch,
        compiler_params=pltpu.CompilerParams(
            collective_id=0, has_side_effects=True, vmem_limit_bytes=62 * 1024 * 1024
        ),
    )(tokens, sel, valid_count.reshape(1, -1), queries, key_matrix, value_matrix, out_grad)
    return pl.pallas_call(
        finish,
        out_shape=(
            shape((SLOTS, HEADS * HEAD), BF),
            shape((SLOTS, HEADS * HEAD), BF),
            shape((ROWS, MODEL // 4), BF),
            shape((HEAD, HEAD), BF),
            shape((HEAD, HEAD), BF),
        ),
        in_specs=[vmem] * 5,
        out_specs=(vmem,) * 5,
        compiler_params=pltpu.CompilerParams(vmem_limit_bytes=6 * 1024 * 1024),
    )(sel, att, dq, rows, wgr)


def solution(mesh):
    in_specs = (
        P("ctx", None), P("ctx"), P(), P("ctx", "tp"), P("ctx", "tp"), P("ctx", "tp"),
        P("ctx", "tp"),
    )
    out_specs = (P("ctx", "tp"),) * 5
    return jax.shard_map(local, mesh=mesh, in_specs=in_specs, out_specs=out_specs, check_vma=False)
```
